512 devices in a mesh: tile: 16 (over z, core), img: 32 (over x, y).
Axes of the slice: x: 4, y: 8, z: 8, core: 2. Of those that a mesh axis runs over, the one named last changes fastest.
Arguments:
- qkv: bfloat16 [32, 16, 8, 32, 1536], P('img', 'tile'), may hold values from -6 to 6
- cotangent: bfloat16 [32, 16, 8, 32, 1024], P('img', 'tile'), may hold values from -48 to 48
- dw_weight: float32 [25, 1536], replicated, may hold values from -1.25 to 1.25
- pw_weight: float32 [32, 1536], replicated, may hold values from -1 to 1
- tile_image: int32 [32, 16], P('img', 'tile'), may hold values from 0 to 8, as said below
- tile_row: int32 [32, 16], P('img', 'tile'), may hold values from 0 to 7, as said below
- tile_col: int32 [32, 16], P('img', 'tile'), may hold values from 0 to 1, as said below
- image_height: int32 [32, 8], P('img'), may hold values from 0 to 8, as said below
- image_width: int32 [32, 8], P('img'), may hold values from 0 to 2, as said below
Outputs:
- grad_qkv: bfloat16 [32, 16, 8, 32, 1536], P('img', 'tile')
- grad_dw: float32 [25, 1536], replicated
- grad_pw: float32 [32, 1536], replicated
The draws below stay inside these ranges and needn't reach their ends.
Inputs may be any that keep to these rules, and one draw needn't show every extreme that they name: Within a group tile_image never falls; each image occupies height * width consecutive tiles; padding tiles come last; the first group holds 8 images of 1 x 2 tiles; the second group holds one image of 8 x 2 tiles. `tile_row`: the tile's row in its image's grid, row-major order; 0 on padding tiles. `tile_col`: the tile's column in its image's grid; 0 on padding tiles. `image_height`: used slots come first; an unused slot has height 0. `image_width`: used slots come first; an unused slot has width 0.
All inputs are finite; a program needn't handle non-finite values.
Results may differ from the reference program's by a relative error of at most 0.005.
Values may be sent and summed in bfloat16 or wider, within the bound.
A program may use at most 64 MiB of HBM per device.

```python
import math
import jax
import jax.numpy as jnp
from jax import lax

HEADS = 16
HD = 32
TILE_H = 8
TILE_W = 32
C3 = 1536
GROUPS = 32
TILES = 16
MAXIMG = 8
HMAX = 8


def layout(key):
    group_keys = jax.random.split(jax.random.fold_in(key, 9173), GROUPS)

    def one_group(group_key, group_index):
        tall_key, wide_key = jax.random.split(group_key)
        heights = jax.random.randint(tall_key, (MAXIMG,), 1, HMAX + 1)
        widths = jax.random.randint(wide_key, (MAXIMG,), 1, 3)
        slot_ids = jnp.arange(MAXIMG)
        heights = jnp.where(group_index == 0, 1, heights)
        widths = jnp.where(group_index == 0, 2, widths)
        heights = jnp.where(group_index == 1, jnp.where(slot_ids == 0, HMAX, 1), heights)
        widths = jnp.where(group_index == 1, 2, widths)
        capacity = jnp.where(group_index <= 1, TILES, TILES - 1)
        run_ends = jnp.cumsum(heights * widths)
        fitting = run_ends <= capacity
        heights = jnp.where(fitting, heights, 0).astype(jnp.int32)
        widths = jnp.where(fitting, widths, 0).astype(jnp.int32)
        tile_areas = heights * widths
        run_ends = jnp.cumsum(tile_areas)
        starts = run_ends - tile_areas
        places = jnp.arange(TILES)
        image_slot = jnp.sum((run_ends[None, :] <= places[:, None]).astype(jnp.int32), axis=1)
        clipped = jnp.minimum(image_slot, MAXIMG - 1)
        within = places - starts[clipped]
        wide_tiles = jnp.maximum(widths[clipped], 1)
        grid_rows = jnp.where(image_slot < MAXIMG, within // wide_tiles, 0)
        grid_cols = jnp.where(image_slot < MAXIMG, within % wide_tiles, 0)
        return (image_slot.astype(jnp.int32), grid_rows.astype(jnp.int32), grid_cols.astype(jnp.int32), heights, widths)
    return jax.vmap(one_group)(group_keys, jnp.arange(GROUPS))


def draw_tile_image(key, part):
    return layout(key)[0]


def draw_tile_row(key, part):
    return layout(key)[1]


def draw_tile_col(key, part):
    return layout(key)[2]


def draw_image_height(key, part):
    return layout(key)[3]


def draw_image_width(key, part):
    return layout(key)[4]


def shard_levels(stream_key, extent, shards, smallest, largest):
    def one(position, parts):
        steps = jax.random.uniform(jax.random.fold_in(jax.random.fold_in(stream_key, 6), position), (parts,), jnp.float32, smallest / len(shards), largest / len(shards))
        return jnp.repeat(jnp.exp(steps), extent[position] // parts).reshape((-1,) + (1,) * (len(extent) - position - 1))

    factor_of = one(*shards[0])
    for cut in shards[1:]:
        factor_of = factor_of * one(*cut)
    return factor_of


def scatter_about(rng, dims, scale, limit, cuts=(), held_as=jnp.bfloat16):
    array = jax.random.normal(rng, dims, jnp.float32) * scale
    if len(cuts) > 0:
        array = shard_levels(rng, dims, cuts, -0.22, 0.18) * array
    return jnp.clip(array, min=-limit, max=limit).astype(held_as)


def setup_inputs(seed: int = 0) -> dict:
    splits = jax.random.split(jax.random.key(seed), 10)
    qkv = scatter_about(splits[0], (GROUPS, TILES, TILE_H, TILE_W, C3), 1.0, 6.0, ((0, 32), (1, 16)))
    cotangent = scatter_about(splits[1], (GROUPS, TILES, TILE_H, TILE_W, 2 * HEADS * HD), 8.0, 48.0, ((0, 32), (1, 16)))
    dw_weight = scatter_about(splits[2], (25, C3), 25 ** -0.5, 1.25, (), jnp.float32)
    pw_weight = scatter_about(splits[3], (HD, C3), HD ** -0.5, 1.0, (), jnp.float32)
    tile_image = draw_tile_image(jax.random.fold_in(splits[9], 71), 0)
    tile_row = draw_tile_row(jax.random.fold_in(splits[9], 71), 0)
    tile_col = draw_tile_col(jax.random.fold_in(splits[9], 71), 0)
    image_height = draw_image_height(jax.random.fold_in(splits[9], 71), 0)
    image_width = draw_image_width(jax.random.fold_in(splits[9], 71), 0)
    return dict(qkv=qkv, cotangent=cotangent, dw_weight=dw_weight, pw_weight=pw_weight, tile_image=tile_image, tile_row=tile_row, tile_col=tile_col, image_height=image_height, image_width=image_width)


PRECISE = lax.Precision.HIGHEST
EPSILON = 1e-06

def widen_tiles(source, is_live, grid_rows, grid_cols, tiles_tall, tiles_wide):
    tile_ids = jnp.arange(TILES).astype(jnp.int32)
    has_left = (is_live & (grid_cols > 0)).astype(jnp.float32)[:, None, None, None]
    has_right = (is_live & (grid_cols < tiles_wide - 1)).astype(jnp.float32)[:, None, None, None]
    has_above = (is_live & (grid_rows > 0)).astype(jnp.float32)[:, None, None, None]
    has_below = (is_live & (grid_rows < tiles_tall - 1)).astype(jnp.float32)[:, None, None, None]
    left_cols = source[jnp.clip(tile_ids - 1, 0, TILES - 1).astype(jnp.int32)][:, :, TILE_W - 2:] * has_left
    right_cols = source[jnp.clip(tile_ids + 1, 0, TILES - 1).astype(jnp.int32)][:, :, :2] * has_right
    widened = jnp.concatenate([left_cols, source, right_cols], axis=2)
    above_rows = widened[jnp.clip(tile_ids - tiles_wide, 0, TILES - 1).astype(jnp.int32)][:, TILE_H - 2:] * has_above
    below_rows = widened[jnp.clip(tile_ids + tiles_wide, 0, TILES - 1).astype(jnp.int32)][:, :2] * has_below
    return jnp.concatenate([above_rows, widened, below_rows], axis=1)

def attend(flat, image_slot):
    chans = HEADS * HD
    queries = jax.nn.relu(flat[..., :chans]).reshape(TILES, -1, HEADS, HD)
    key_rows = jax.nn.relu(flat[..., chans:2 * chans]).reshape(TILES, -1, HEADS, HD)
    values = flat[..., 2 * chans:].reshape(TILES, -1, HEADS, HD)
    onehot = (image_slot[:, None] == jnp.arange(MAXIMG)[None, :]).astype(jnp.float32)
    states = jnp.einsum('tphi,tphj->tihj', key_rows, values, precision=PRECISE)
    states = jnp.einsum('tm,tihj->mihj', onehot, states, precision=PRECISE)
    states = jnp.einsum('tm,mihj->tihj', onehot, states, precision=PRECISE)
    key_sums = jnp.einsum('tm,thi->mhi', onehot, lax.optimization_barrier(jnp.sum(key_rows, axis=1)), precision=PRECISE)
    key_sums = jnp.einsum('tm,mhi->thi', onehot, key_sums, precision=PRECISE)
    numerator = jnp.einsum('tphi,tihj->tphj', queries, states, precision=PRECISE)
    denominator = jnp.einsum('tphi,thi->tph', queries, key_sums, precision=PRECISE) + EPSILON
    return (numerator / denominator[..., None]).reshape(TILES, -1, chans)

def group_forward(source, dw_weight, pw_weight, image_slot, grid_rows, grid_cols, tiles_tall, tiles_wide):
    is_live = image_slot < MAXIMG
    padded = widen_tiles(source, is_live, grid_rows, grid_cols, tiles_tall, tiles_wide)
    mixed_dw = jnp.zeros_like(source)
    for row_off in range(5):
        for col_off in range(5):
            mixed_dw = mixed_dw + padded[:, row_off:row_off + TILE_H, col_off:col_off + TILE_W] * dw_weight[row_off * 5 + col_off]
    grouped = mixed_dw.reshape(TILES, TILE_H * TILE_W, 3 * HEADS, HD)
    merged = jnp.einsum('tpgi,igo->tpgo', grouped, pw_weight.reshape(HD, 3 * HEADS, HD), precision=PRECISE)
    merged = merged.reshape(TILES, TILE_H * TILE_W, C3)
    central = source.reshape(TILES, TILE_H * TILE_W, C3)
    return jnp.concatenate([attend(central, image_slot), attend(merged, image_slot)], axis=-1)

def reference(qkv, cotangent, dw_weight, pw_weight, tile_image, tile_row, tile_col, image_height, image_width):

    def per_group(running, packed):
        source, cot_tiles, image_slot, grid_rows, grid_cols, heights, widths = packed
        slot_index = jnp.minimum(image_slot, MAXIMG - 1).astype(jnp.int32)
        tiles_tall = heights[slot_index]
        tiles_wide = widths[slot_index]
        is_live = (image_slot < MAXIMG).astype(jnp.float32)[:, None, None, None]
        source = source.astype(jnp.float32) * is_live

        def forward_fn(src, dwk, pwk):
            return group_forward(src, dwk, pwk, image_slot, grid_rows, grid_cols, tiles_tall, tiles_wide)
        result, pullback = jax.vjp(forward_fn, source, dw_weight, pw_weight)
        grad_src, grad_dwk, grad_pwk = pullback(cot_tiles.astype(jnp.float32).reshape(result.shape))
        grad_src = grad_src * is_live
        return ((running[0] + grad_dwk, running[1] + grad_pwk), grad_src.astype(jnp.bfloat16))
    zeros_init = (jnp.zeros_like(dw_weight), jnp.zeros_like(pw_weight))
    (grad_dwk, grad_pwk), grad_src = lax.scan(per_group, zeros_init, (qkv, cotangent, tile_image, tile_row, tile_col, image_height, image_width))
    weight_norm = 1.0 / math.sqrt(GROUPS * TILES * TILE_H * TILE_W)
    return (grad_src, grad_dwk * weight_norm, grad_pwk * weight_norm)
```

```python
import functools
import math

import jax
import jax.numpy as jnp
from jax import lax
from jax.experimental import pallas as pl
from jax.experimental.pallas import tpu as pltpu
from jax.sharding import PartitionSpec as P

MESH = pl.DeviceIdType.MESH
F32, BF16 = jnp.float32, jnp.bfloat16
EPSILON = 1e-06
TALL, BROAD, LANES, HD = 8, 32, 128, 32
POS = TALL * BROAD
PITCH = 48
NB = 12
TILES = 16
STATE_DT = F32
GRAD_DT = F32


def split(x):
    hi = x.astype(BF16)
    return hi, (x - hi.astype(F32)).astype(BF16)


def dot(a, b, dims):
    return lax.dot_general(a, b, (dims, ((), ())), preferred_element_type=F32)


NN, NT, TN = ((1,), (0,)), ((1,), (1,)), ((0,), (0,))


def mm(a, b, dims):
    out = dot(a[0], b[0], dims)
    if len(b) > 1:
        out = out + dot(a[0], b[1], dims)
    if len(a) > 1:
        out = out + dot(a[1], b[0], dims)
    return out


def kernel(nx, ny, norm, qkv, cot, dw, pw, t_img, t_row, t_col, im_h, im_w, out, gdw, gpw, *scratch):
    (x_raw, x_live, c_in, dwk, pwk, pad, pad2, mix, mrg, gsrc, gmrg, o_blk,
     st_send, st_recv, st_tot, st_out,
     cols_f, corner_f, cols_s, corner_s, rows_s, rows_r, cols_r, corner_r,
     dw_tmp, g_send, g_recv, g_x, g_y, g_tot, g_fin,
     in_sem, out_sem, rs_s, rs_r, ag_s, ag_r, h_s, h_r, gr_s, gr_r, gx_s, gx_r, gy_s, gy_r, ga_s, ga_r) = scratch
    me = lax.axis_index("tile")
    im = lax.axis_index("img")
    mx, my = im // ny, im % ny

    def peer(d):
        return (me + d + TILES) % TILES

    def x_peer(d):
        return ((mx + d) % nx) * ny + my

    def y_peer(d):
        return mx * ny + (my + d) % ny

    def push(src, dst, ssem, rsem, where):
        return pltpu.make_async_remote_copy(
            src_ref=src, dst_ref=dst, send_sem=ssem, recv_sem=rsem, device_id=where, device_id_type=MESH
        )

    def loop(lo, hi, body):
        lax.fori_loop(lo, hi, lambda i, carry: (body(i), carry)[1], 0)

    def in_copies():
        copies = []
        for c in range(NB):
            lanes = pl.ds(c * LANES, LANES)
            copies.append(pltpu.make_async_copy(qkv.at[:, lanes], x_raw.at[c], in_sem.at[c]))
            copies.append(pltpu.make_async_copy(dw.at[:, lanes], dwk.at[c], in_sem.at[NB + c]))
            copies.append(pltpu.make_async_copy(pw.at[:, lanes], pwk.at[c], in_sem.at[2 * NB + c]))
        for c in range(8):
            lanes = pl.ds(c * LANES, LANES)
            copies.append(pltpu.make_async_copy(cot.at[:, lanes], c_in.at[c], in_sem.at[3 * NB + c]))
        return copies

    for copy in in_copies():
        copy.start()

    barrier = pltpu.get_barrier_semaphore()
    loop(1, TILES, lambda d: pl.semaphore_signal(
        barrier, inc=1, device_id={"tile": peer(d)}, device_id_type=MESH))
    if nx > 1:
        loop(1, nx, lambda d: pl.semaphore_signal(
            barrier, inc=1, device_id={"img": x_peer(d)}, device_id_type=MESH))
    if ny > 1:
        loop(1, ny, lambda d: pl.semaphore_signal(
            barrier, inc=1, device_id={"img": y_peer(d)}, device_id_type=MESH))

    slots = im_h.shape[1]
    slot = t_img[0, 0]
    one, zero = jnp.float32(1), jnp.float32(0)

    def flag(cond):
        return jnp.where(cond, one, zero)

    tall, wide, end = jnp.int32(0), jnp.int32(0), jnp.int32(0)
    ends = []
    for m in range(slots):
        tall = tall + jnp.where(slot == m, im_h[0, m], 0)
        wide = wide + jnp.where(slot == m, im_w[0, m], 0)
        end = end + im_h[0, m] * im_w[0, m]
        ends.append(end)
    live = flag(slot < slots)
    has_l = live * flag(t_col[0, 0] > 0)
    has_r = live * flag(t_col[0, 0] < wide - 1)
    has_a = live * flag(t_row[0, 0] > 0)
    has_b = live * flag(t_row[0, 0] < tall - 1)
    thin = flag(wide == 1)
    a1, a2, b1, b2 = has_a * thin, has_a * (one - thin), has_b * thin, has_b * (one - thin)
    keep = [zero] * TILES
    for s in range(1, TILES):
        joined = one
        for m in range(slots):
            joined = joined * flag(ends[m] != s)
        keep[s] = joined

    lane_head = lax.broadcasted_iota(jnp.int32, (LANES, LANES), 1) // HD
    row_head = lax.broadcasted_iota(jnp.int32, (LANES, LANES), 0) // HD
    same_head = flag(lane_head == row_head)
    same_bf = (same_head.astype(BF16),)

    def expand(compact):
        return jnp.concatenate([compact] * 4, axis=0) * same_head

    def compact(full):
        masked = full * same_head
        return masked[0:32] + masked[32:64] + masked[64:96] + masked[96:128]

    def place(c):
        pltpu.make_async_copy(qkv.at[:, pl.ds(0, LANES)], x_raw.at[c], in_sem.at[c]).wait()
        for y in range(TALL):
            rows = x_raw[c, y * BROAD:(y + 1) * BROAD, :].astype(F32) * live
            pad[c, pl.ds((2 + y) * PITCH + 8, BROAD), :] = rows
            x_live[c, y * BROAD:(y + 1) * BROAD, :] = rows.astype(BF16)

    loop(0, NB, place)

    def stage(c, field, k):
        for side, first in ((0, 38), (1, 8)):
            for i in range(2):
                cols_f[i * 8:(i + 1) * 8, :] = field[c, pl.ds(2 * PITCH + first + i, 8, stride=PITCH), :]
            cols_s[k, side, c] = cols_f[...].astype(BF16)

    def stage_corners(field, k):
        for side, row, first in ((0, 8, 38), (1, 2, 8)):
            for c in range(NB):
                for i in range(2):
                    corner_f[4 * c + 2 * i:4 * c + 2 * i + 2, :] = field[c, pl.ds((row + i) * PITCH + first, 2), :]
            corner_s[k, side] = corner_f[...].astype(BF16)

    def halo(k):
        if k == 0:
            bottom, top = x_raw.at[:, pl.ds(POS - 64, 64)], x_raw.at[:, pl.ds(0, 64)]
        else:
            bottom, top = rows_s.at[0], rows_s.at[1]
        plan = [
            (bottom, rows_r.at[k, 0], 1), (top, rows_r.at[k, 1], -1),
            (bottom, rows_r.at[k, 2], 2), (top, rows_r.at[k, 3], -2),
            (cols_s.at[k, 0], cols_r.at[k, 0], 1), (cols_s.at[k, 1], cols_r.at[k, 1], -1),
            (corner_s.at[k, 0], corner_r.at[k, 0], 3), (corner_s.at[k, 1], corner_r.at[k, 1], -3),
        ]
        return [
            push(src, dst, h_s.at[k, i], h_r.at[k, i], {"tile": peer(step)})
            for i, (src, dst, step) in enumerate(plan)
        ]

    def land_corners(field, k):
        for side, row, first, has in ((0, 0, 6, has_a * has_l), (1, 10, 40, has_b * has_r)):
            corner_f[...] = corner_r[k, side].astype(F32) * has
            for c in range(NB):
                for i in range(2):
                    field[c, pl.ds((row + i) * PITCH + first, 2), :] = corner_f[4 * c + 2 * i:4 * c + 2 * i + 2, :]

    def land(c, field, k):
        above1, below1 = rows_r[k, 0, c].astype(F32), rows_r[k, 1, c].astype(F32)
        above2, below2 = rows_r[k, 2, c].astype(F32), rows_r[k, 3, c].astype(F32)
        above = above1 * a1 + above2 * a2
        below = below1 * b1 + below2 * b2
        for i in range(2):
            cut = slice(i * BROAD, (i + 1) * BROAD)
            field[c, pl.ds(i * PITCH + 8, BROAD), :] = above[cut]
            field[c, pl.ds((10 + i) * PITCH + 8, BROAD), :] = below[cut]
            field[c, pl.ds(i * PITCH + 40, 2), :] = above1[i * BROAD:i * BROAD + 2] * (has_a * has_r)
            field[c, pl.ds((10 + i) * PITCH + 6, 2), :] = below1[i * BROAD + 30:i * BROAD + 32] * (has_b * has_l)
        left = cols_r[k, 0, c].astype(F32) * has_l
        right = cols_r[k, 1, c].astype(F32) * has_r
        for i in range(2):
            field[c, pl.ds(2 * PITCH + 6 + i, 8, stride=PITCH), :] = left[i * 8:(i + 1) * 8]
            field[c, pl.ds(2 * PITCH + 40 + i, 8, stride=PITCH), :] = right[i * 8:(i + 1) * 8]

    def convolve(c, field, flipped, put):
        taps = [dwk[c, pl.ds(t, 1), :] for t in range(25)]
        for y in range(0, TALL, 2):
            acc = [None, None]
            for r in range(6):
                for b in range(5):
                    rows = field[c, pl.ds((y + r) * PITCH + 6 + b, BROAD), :]
                    for k in range(2):
                        a = r - k
                        if 0 <= a < 5:
                            t = 24 - (5 * a + b) if flipped else 5 * a + b
                            term = rows * taps[t]
                            acc[k] = term if acc[k] is None else acc[k] + term
            for k in range(2):
                put(c, y + k, acc[k])

    def post_state(e, j, state, key_sum):
        if STATE_DT == F32:
            tail = jnp.broadcast_to(key_sum, (8, LANES))
        else:
            row = lax.broadcasted_iota(jnp.int32, (8, LANES), 0)
            high = key_sum.astype(BF16).astype(F32)
            tail = jnp.where(row == 0, high, jnp.where(row == 1, key_sum - high, 0.0))
        for r in range(4):
            st_send[e, 4 * j + r] = jnp.concatenate([state[8 * r:8 * r + 8], tail], axis=0).astype(STATE_DT)

    def rs(e, d):
        p = peer(d)
        return push(st_send.at[e, p], st_recv.at[e, me], rs_s.at[e, d], rs_r.at[e, me], {"tile": p})

    def rs_from(e, d):
        p = peer(d)
        return push(st_send.at[e, p], st_recv.at[e, p], rs_s.at[e, d], rs_r.at[e, p], {"tile": p})

    def ag(e, d):
        p = peer(d)
        return push(st_tot.at[e, p], st_out.at[e, me], ag_s.at[e, d], ag_r.at[e, me], {"tile": p})

    def ag_from(e, d):
        p = peer(d)
        return push(st_tot.at[e, p], st_out.at[e, p], ag_s.at[e, d], ag_r.at[e, p], {"tile": p})

    def scatter(e):
        loop(1, TILES, lambda d: rs(e, d).start())
        st_recv[e, me] = st_send[e, me]

    def total(e):
        loop(1, TILES, lambda d: rs_from(e, d).wait_recv())
        run = st_recv[e, 0].astype(F32)
        runs = [run]
        for s in range(1, TILES):
            run = run * keep[s] + st_recv[e, s].astype(F32)
            runs.append(run)
        for s in range(TILES - 1, -1, -1):
            if s < TILES - 1:
                run = run * keep[s + 1] + runs[s] * (one - keep[s + 1])
            if STATE_DT == F32:
                st_tot[e, s] = run
            else:
                row = lax.broadcasted_iota(jnp.int32, (8, LANES), 0)
                key_sum = run[8:9] + run[9:10]
                high = key_sum.astype(BF16).astype(F32)
                tail = jnp.where(row == 0, high, jnp.where(row == 1, key_sum - high, 0.0))
                st_tot[e, s] = jnp.concatenate([run[0:8], tail], axis=0).astype(STATE_DT)
        loop(1, TILES, lambda d: ag(e, d).start())
        st_out[e, me] = st_tot[e, me]

    def gather(e):
        loop(1, TILES, lambda d: ag_from(e, d).wait_recv())

    def get_state(e, j):
        parts = [st_out[e, 4 * j + r].astype(F32) for r in range(4)]
        state = expand(jnp.concatenate([part[0:8] for part in parts], axis=0))
        key_sum = parts[0][8:9]
        if STATE_DT != F32:
            key_sum = key_sum + parts[0][9:10]
        return (split(state) if STATE_DT == F32 else (state.astype(BF16),)), key_sum

    def terms(scale, j):
        if scale == 0:
            raw = x_live[j]
            return raw.astype(F32), (raw,)
        raw = mrg[j]
        return raw, split(raw)

    def relu_terms(scale, j):
        raw, parts = terms(scale, j)
        rect = jnp.maximum(raw, 0.0)
        return raw, rect, ((rect.astype(BF16),) if scale == 0 else split(rect))

    def states(scale):
        def body(j):
            _, rect, keys = relu_terms(scale, 4 + j)
            _, values = terms(scale, 8 + j)
            post_state(scale, j, compact(mm(keys, values, TN)), jnp.sum(rect, axis=0, keepdims=True))
        loop(0, 4, body)

    def attend(scale, grads):
        def body(j):
            state, key_sum = get_state(scale, j)
            raw, rect, queries = relu_terms(scale, j)
            den = mm(split(rect * key_sum), same_bf, NN) + EPSILON
            inverse = 1.0 / den
            num = mm(queries, state, NN)
            grad = c_in[4 * scale + j].astype(F32)
            grad_num = grad * inverse
            grad_den = -mm(split(grad_num * num), same_bf, NN) * inverse
            grad_parts = split(grad_num)
            grad_query = mm(grad_parts, state, NT) + grad_den * key_sum
            grads[j] = jnp.where(raw > 0, grad_query, 0.0)
            post_state(2 + scale, j, compact(mm(queries, grad_parts, TN)),
                       jnp.sum(rect * grad_den, axis=0, keepdims=True))
        loop(0, 4, body)

    def attend_back(scale, grads):
        def body(j):
            state, key_sum = get_state(2 + scale, j)
            raw, _, keys = relu_terms(scale, 4 + j)
            _, values = terms(scale, 8 + j)
            grad_key = mm(values, state, NT) + key_sum
            grads[4 + j] = jnp.where(raw > 0, grad_key, 0.0)
            grads[8 + j] = mm(keys, state, NN)
        loop(0, 4, body)

    loop(0, NB, lambda c: stage(c, pad, 0))
    stage_corners(pad, 0)
    states(0)
    pl.semaphore_wait(barrier, (TILES - 1) + (nx - 1) + (ny - 1))
    halo_in = halo(0)
    for copy in halo_in:
        copy.start()
    scatter(0)
    for c in range(NB):
        lanes = pl.ds(c * LANES, LANES)
        pltpu.make_async_copy(dw.at[:, lanes], dwk.at[c], in_sem.at[NB + c]).wait()
        pltpu.make_async_copy(pw.at[:, lanes], pwk.at[c], in_sem.at[2 * NB + c]).wait()
    for c in range(8):
        pltpu.make_async_copy(cot.at[:, pl.ds(c * LANES, LANES)], c_in.at[c], in_sem.at[3 * NB + c]).wait()
    for copy in halo_in:
        copy.wait_recv()
    land_corners(pad, 0)

    def put_mix(c, y, rows):
        mix[c, y * BROAD:(y + 1) * BROAD, :] = rows

    def forward(c):
        land(c, pad, 0)
        convolve(c, pad, False, put_mix)
        weight = split(expand(pwk[c]))
        mrg[c] = mm(split(mix[c]), weight, NN)

    loop(0, NB, forward)
    states(1)
    scatter(1)
    total(0)
    gather(0)
    attend(0, gsrc)
    scatter(2)
    total(1)
    gather(1)
    attend(1, gmrg)
    scatter(3)
    total(2)
    gather(2)
    attend_back(0, gsrc)
    total(3)
    gather(3)
    attend_back(1, gmrg)

    dw_tmp[...] = jnp.zeros((32, LANES), F32)

    def backward(c):
        weight = split(expand(pwk[c]))
        grads = split(gmrg[c] * live)
        grad_mix = mm(grads, weight, NT)
        for y in range(TALL):
            pad2[c, pl.ds((2 + y) * PITCH + 8, BROAD), :] = grad_mix[y * BROAD:(y + 1) * BROAD]
        rows_s[0, c] = grad_mix[POS - 64:].astype(BF16)
        rows_s[1, c] = grad_mix[:64].astype(BF16)
        stage(c, pad2, 1)
        grad_pw = compact(mm(split(mix[c]), grads, TN))
        for b in range(5):
            acc = [None] * 5
            for r in range(12):
                rows = pad[c, pl.ds(r * PITCH + 6 + b, BROAD), :]
                for a in range(5):
                    y = r - a
                    if 0 <= y < TALL:
                        term = rows * pad2[c, pl.ds((2 + y) * PITCH + 8, BROAD), :]
                        acc[a] = term if acc[a] is None else acc[a] + term
            for a in range(5):
                t = 5 * a + b
                dw_tmp[t:t + 1, :] = jnp.sum(acc[a], axis=0, keepdims=True)
        for i in range(2):
            g_send[4 * c + i] = grad_pw[16 * i:16 * i + 16].astype(GRAD_DT)
            g_send[4 * c + 2 + i] = dw_tmp[16 * i:16 * i + 16, :].astype(GRAD_DT)

    loop(0, NB, backward)
    stage_corners(pad2, 1)

    def grad_rs(d):
        p = peer(d)
        return push(g_send.at[pl.ds(3 * p, 3)], g_recv.at[me], gr_s.at[d], gr_r.at[me], {"tile": p})

    def grad_rs_from(d):
        p = peer(d)
        return push(g_send.at[pl.ds(3 * p, 3)], g_recv.at[p], gr_s.at[d], gr_r.at[p], {"tile": p})

    loop(1, TILES, lambda d: grad_rs(d).start())
    g_recv[me] = g_send[pl.ds(3 * me, 3)]
    halo_back = halo(1)
    for copy in halo_back:
        copy.start()

    def add_up(ref, count):
        acc = ref[0].astype(F32)
        for s in range(1, count):
            acc = acc + ref[s].astype(F32)
        return acc

    loop(1, TILES, lambda d: grad_rs_from(d).wait_recv())
    g_x[mx] = add_up(g_recv, TILES)

    def grad_x(d, slot_of):
        return push(g_x.at[mx], g_x.at[slot_of], gx_s.at[d], gx_r.at[slot_of], {"img": x_peer(d)})

    def grad_y(d, slot_of):
        return push(g_y.at[my], g_y.at[slot_of], gy_s.at[d], gy_r.at[slot_of], {"img": y_peer(d)})

    if nx > 1:
        loop(1, nx, lambda d: grad_x(d, mx).start())
    for copy in halo_back:
        copy.wait_recv()
    land_corners(pad2, 1)

    def put_out(c, y, rows):
        rows = (rows + gsrc[c, y * BROAD:(y + 1) * BROAD, :]) * live
        o_blk[c, y * BROAD:(y + 1) * BROAD, :] = rows.astype(BF16)

    def out_copy(c):
        lanes = pl.ds(pl.multiple_of(c * LANES, LANES), LANES)
        return pltpu.make_async_copy(o_blk.at[c], out.at[:, lanes], out_sem.at[c])

    def last(c):
        land(c, pad2, 1)
        convolve(c, pad2, True, put_out)
        out_copy(c).start()

    loop(0, 4, last)
    if nx > 1:
        loop(1, nx, lambda d: grad_x(d, (mx + d) % nx).wait_recv())
    g_y[my] = add_up(g_x, nx)
    if ny > 1:
        loop(1, ny, lambda d: grad_y(d, my).start())
    loop(4, NB, last)
    if ny > 1:
        loop(1, ny, lambda d: grad_y(d, (my + d) % ny).wait_recv())
    g_tot[...] = (add_up(g_y, ny) * norm).astype(GRAD_DT)

    def grad_ag(d, slot_of):
        p = peer(d)
        return push(g_tot, g_fin.at[pl.ds(3 * slot_of, 3)], ga_s.at[d], ga_r.at[slot_of], {"tile": p})

    loop(1, TILES, lambda d: grad_ag(d, me).start())
    g_fin[pl.ds(3 * me, 3)] = g_tot[...]

    for copy in halo_in + halo_back:
        copy.wait_send()

    def drain(d):
        for e in range(4):
            rs(e, d).wait_send()
            ag(e, d).wait_send()
        grad_rs(d).wait_send()

    loop(1, TILES, drain)
    if nx > 1:
        loop(1, nx, lambda d: grad_x(d, mx).wait_send())
    if ny > 1:
        loop(1, ny, lambda d: grad_y(d, my).wait_send())
    loop(0, NB, lambda c: out_copy(c).wait())
    loop(1, TILES, lambda d: grad_ag(d, peer(d)).wait_recv())
    for c in range(NB):
        lanes = slice(c * LANES, (c + 1) * LANES)
        for i in range(2):
            gpw[16 * i:16 * i + 16, lanes] = g_fin[4 * c + i].astype(F32)
        gdw[0:16, lanes] = g_fin[4 * c + 2].astype(F32)
        gdw[16:25, lanes] = g_fin[4 * c + 3].astype(F32)[0:9]
    loop(1, TILES, lambda d: grad_ag(d, me).wait_send())


def local(nx, ny, qkv, cotangent, dw_weight, pw_weight, tile_image, tile_row, tile_col, image_height, image_width):
    channels, inner = qkv.shape[4], cotangent.shape[4]
    norm = 1.0 / math.sqrt(POS * lax.axis_size("tile") * lax.axis_size("img"))
    dma = pltpu.SemaphoreType.DMA
    vm = pltpu.VMEM
    any_spec = pl.BlockSpec(memory_space=pl.ANY)
    smem = pl.BlockSpec(memory_space=pltpu.SMEM)
    vmem = pl.BlockSpec(memory_space=pltpu.VMEM)
    scratch = [
        vm((NB, POS, LANES), BF16), vm((NB, POS, LANES), BF16), vm((8, POS, LANES), BF16),
        vm((NB, 25, LANES), F32), vm((NB, HD, LANES), F32),
        vm((NB, 12 * PITCH, LANES), F32), vm((NB, 12 * PITCH, LANES), F32),
        vm((NB, POS, LANES), F32), vm((NB, POS, LANES), F32), vm((NB, POS, LANES), F32), vm((NB, POS, LANES), F32),
        vm((NB, POS, LANES), BF16),
        vm((4, TILES, 16, LANES), STATE_DT), vm((4, TILES, 16, LANES), STATE_DT),
        vm((4, TILES, 16, LANES), STATE_DT), vm((4, TILES, 16, LANES), STATE_DT),
        vm((16, LANES), F32), vm((48, LANES), F32),
        vm((2, 2, NB, 16, LANES), BF16), vm((2, 2, 48, LANES), BF16), vm((2, NB, 64, LANES), BF16),
        vm((2, 4, NB, 64, LANES), BF16), vm((2, 2, NB, 16, LANES), BF16), vm((2, 2, 48, LANES), BF16),
        vm((32, LANES), F32),
        vm((48, 16, LANES), GRAD_DT), vm((TILES, 3, 16, LANES), GRAD_DT),
        vm((nx, 3, 16, LANES), F32), vm((ny, 3, 16, LANES), F32),
        vm((3, 16, LANES), GRAD_DT), vm((48, 16, LANES), GRAD_DT),
        dma((3 * NB + 8,)), dma((NB,)),
        dma((4, TILES)), dma((4, TILES)), dma((4, TILES)), dma((4, TILES)),
        dma((2, 8)), dma((2, 8)),
        dma((TILES,)), dma((TILES,)), dma((max(nx, 2),)), dma((max(nx, 2),)), dma((max(ny, 2),)), dma((max(ny, 2),)),
        dma((TILES,)), dma((TILES,)),
    ]
    grad, grad_dw, grad_pw = pl.pallas_call(
        functools.partial(kernel, nx, ny, norm),
        out_shape=(
            jax.ShapeDtypeStruct((POS, channels), BF16),
            jax.ShapeDtypeStruct((25, channels), F32),
            jax.ShapeDtypeStruct((HD, channels), F32),
        ),
        in_specs=[any_spec] * 4 + [smem] * 5,
        out_specs=(any_spec, vmem, vmem),
        scratch_shapes=scratch,
        compiler_params=pltpu.CompilerParams(
            collective_id=0, has_side_effects=True, vmem_limit_bytes=60 * 1024 * 1024
        ),
        name="linear_attention",
    )(
        qkv.reshape(POS, channels), cotangent.reshape(POS, inner), dw_weight, pw_weight,
        tile_image, tile_row, tile_col, image_height, image_width,
    )
    return grad.reshape(qkv.shape), grad_dw, grad_pw


def solution(mesh):
    placed = (
        P("img", "tile", None, None, None),
        P("img", "tile", None, None, None),
        P(),
        P(),
        P("img", "tile"),
        P("img", "tile"),
        P("img", "tile"),
        P("img", None),
        P("img", None),
    )
    count = mesh.shape["img"]
    nx = {32: 4, 4: 2}.get(count, 1)
    return jax.shard_map(
        functools.partial(local, nx, count // nx),
        mesh=mesh,
        in_specs=placed,
        out_specs=(P("img", "tile", None, None, None), P(), P()),
        check_vma=False,
    )
```

```python
import functools
import math

import jax
import jax.numpy as jnp
from jax import lax
from jax.experimental import pallas as pl
from jax.experimental.pallas import tpu as pltpu
from jax.sharding import PartitionSpec as P

MESH = pl.DeviceIdType.MESH
F32, BF16 = jnp.float32, jnp.bfloat16
EPSILON = 1e-06
TALL, BROAD, LANES, HD = 8, 32, 128, 32
POS = TALL * BROAD
PITCH = 48
NB = 12
TILES = 16
STATE_DT = BF16
GRAD_DT = BF16
QB = 4


def split(x):
    hi = x.astype(BF16)
    return hi, (x - hi.astype(F32)).astype(BF16)


def dot(a, b, dims):
    return lax.dot_general(a, b, (dims, ((), ())), preferred_element_type=F32)


NN, NT, TN = ((1,), (0,)), ((1,), (1,)), ((0,), (0,))


def mm(a, b, dims):
    out = dot(a[0], b[0], dims)
    if len(b) > 1:
        out = out + dot(a[0], b[1], dims)
    if len(a) > 1:
        out = out + dot(a[1], b[0], dims)
    return out


def kernel(nx, ny, norm, qkv, cot, dw, pw, t_img, t_row, t_col, im_h, im_w, out, g_fin, *scratch):
    (x_raw, x_live, c_in, dwk, pwk, pad, pad2, mix, mrg, gsrc, gmrg, o_blk,
     st_send, st_recv, st_tot, st_out,
     cols_f, corner_f, cols_s, corner_s, rows_s, rows_r, cols_r, corner_r,
     dw_tmp, g_send, g_recv, g_x, g_y, g_tot, g_all,
     in_sem, out_sem, rs_s, rs_r, ag_s, ag_r, h_s, h_r, gr_s, gr_r, gx_s, gx_r, gy_s, gy_r, ga_s, ga_r) = scratch
    me = lax.axis_index("tile")
    im = lax.axis_index("img")
    mx, my = im // ny, im % ny

    def peer(d):
        return (me + d + TILES) % TILES

    def x_peer(d):
        return ((mx + d) % nx) * ny + my

    def y_peer(d):
        return mx * ny + (my + d) % ny

    def push(src, dst, ssem, rsem, where):
        return pltpu.make_async_remote_copy(
            src_ref=src, dst_ref=dst, send_sem=ssem, recv_sem=rsem, device_id=where, device_id_type=MESH
        )

    def loop(lo, hi, body):
        lax.fori_loop(lo, hi, lambda i, carry: (body(i), carry)[1], 0)

    def in_copies():
        copies = []
        for c in range(NB):
            lanes = pl.ds(c * LANES, LANES)
            copies.append(pltpu.make_async_copy(qkv.at[:, lanes], x_raw.at[c], in_sem.at[c]))
            copies.append(pltpu.make_async_copy(dw.at[:, lanes], dwk.at[c], in_sem.at[NB + c]))
            copies.append(pltpu.make_async_copy(pw.at[:, lanes], pwk.at[c], in_sem.at[2 * NB + c]))
        for c in range(8):
            lanes = pl.ds(c * LANES, LANES)
            copies.append(pltpu.make_async_copy(cot.at[:, lanes], c_in.at[c], in_sem.at[3 * NB + c]))
        return copies

    for copy in in_copies():
        copy.start()

    barrier = pltpu.get_barrier_semaphore()
    loop(1, TILES, lambda d: pl.semaphore_signal(
        barrier, inc=1, device_id={"tile": peer(d)}, device_id_type=MESH))
    if nx > 1:
        loop(1, nx, lambda d: pl.semaphore_signal(
            barrier, inc=1, device_id={"img": x_peer(d)}, device_id_type=MESH))
    if ny > 1:
        loop(1, ny, lambda d: pl.semaphore_signal(
            barrier, inc=1, device_id={"img": y_peer(d)}, device_id_type=MESH))

    slots = im_h.shape[1]
    slot = t_img[0, 0]
    one, zero = jnp.float32(1), jnp.float32(0)

    def flag(cond):
        return jnp.where(cond, one, zero)

    tall, wide, end = jnp.int32(0), jnp.int32(0), jnp.int32(0)
    ends = []
    for m in range(slots):
        tall = tall + jnp.where(slot == m, im_h[0, m], 0)
        wide = wide + jnp.where(slot == m, im_w[0, m], 0)
        end = end + im_h[0, m] * im_w[0, m]
        ends.append(end)
    live = flag(slot < slots)
    has_l = live * flag(t_col[0, 0] > 0)
    has_r = live * flag(t_col[0, 0] < wide - 1)
    has_a = live * flag(t_row[0, 0] > 0)
    has_b = live * flag(t_row[0, 0] < tall - 1)
    thin = flag(wide == 1)
    a1, a2, b1, b2 = has_a * thin, has_a * (one - thin), has_b * thin, has_b * (one - thin)
    keep = [zero] * TILES
    for s in range(1, TILES):
        joined = one
        for m in range(slots):
            joined = joined * flag(ends[m] != s)
        keep[s] = joined

    lane_head = lax.broadcasted_iota(jnp.int32, (LANES, LANES), 1) // HD
    row_head = lax.broadcasted_iota(jnp.int32, (LANES, LANES), 0) // HD
    same_head = flag(lane_head == row_head)
    same_bf = (same_head.astype(BF16),)

    def expand(compact):
        return jnp.concatenate([compact] * 4, axis=0) * same_head

    def compact(full):
        masked = full * same_head
        return masked[0:32] + masked[32:64] + masked[64:96] + masked[96:128]

    def place(c):
        pltpu.make_async_copy(qkv.at[:, pl.ds(0, LANES)], x_raw.at[c], in_sem.at[c]).wait()
        for y in range(TALL):
            rows = x_raw[c, y * BROAD:(y + 1) * BROAD, :].astype(F32) * live
            pad[c, pl.ds((2 + y) * PITCH + 8, BROAD), :] = rows
            x_live[c, y * BROAD:(y + 1) * BROAD, :] = rows.astype(BF16)

    loop(0, NB, place)

    def stage(c, field, k):
        for side, first in ((0, 38), (1, 8)):
            for i in range(2):
                cols_f[i * 8:(i + 1) * 8, :] = field[c, pl.ds(2 * PITCH + first + i, 8, stride=PITCH), :]
            cols_s[k, side, c] = cols_f[...].astype(BF16)

    def stage_corners(field, k, lo, hi):
        for side, row, first in ((0, 8, 38), (1, 2, 8)):
            for c in range(lo, hi):
                for i in range(2):
                    corner_f[4 * c + 2 * i:4 * c + 2 * i + 2, :] = field[c, pl.ds((row + i) * PITCH + first, 2), :]
            corner_s[k, side, 4 * lo:4 * hi] = corner_f[4 * lo:4 * hi, :].astype(BF16)

    def halo(k, lo, hi):
        blocks, group = pl.ds(lo, hi - lo), int(lo == 0)
        corner = pl.ds(4 * lo, 4 * (hi - lo))
        if k == 0:
            bottom, top = x_raw.at[blocks, pl.ds(POS - 64, 64)], x_raw.at[blocks, pl.ds(0, 64)]
        else:
            bottom, top = rows_s.at[0, blocks], rows_s.at[1, blocks]
        plan = [
            (cols_s.at[k, 0, blocks], cols_r.at[k, 0, blocks], 1), (cols_s.at[k, 1, blocks], cols_r.at[k, 1, blocks], -1),
            (corner_s.at[k, 0, corner], corner_r.at[k, 0, corner], 3),
            (corner_s.at[k, 1, corner], corner_r.at[k, 1, corner], -3),
            (bottom, rows_r.at[k, 2, blocks], 2), (top, rows_r.at[k, 3, blocks], -2),
            (bottom, rows_r.at[k, 0, blocks], 1), (top, rows_r.at[k, 1, blocks], -1),
        ]
        return [
            push(src, dst, h_s.at[k, group, i], h_r.at[k, group, i], {"tile": peer(step)})
            for i, (src, dst, step) in enumerate(plan)
        ]

    def land_corners(field, k, lo, hi):
        for side, row, first, has in ((0, 0, 6, has_a * has_l), (1, 10, 40, has_b * has_r)):
            corner_f[4 * lo:4 * hi, :] = corner_r[k, side, 4 * lo:4 * hi].astype(F32) * has
            for c in range(lo, hi):
                for i in range(2):
                    field[c, pl.ds((row + i) * PITCH + first, 2), :] = corner_f[4 * c + 2 * i:4 * c + 2 * i + 2, :]

    def land_rows(c, field, k):
        above1, below1 = rows_r[k, 0, c].astype(F32), rows_r[k, 1, c].astype(F32)
        above2, below2 = rows_r[k, 2, c].astype(F32), rows_r[k, 3, c].astype(F32)
        above = above1 * a1 + above2 * a2
        below = below1 * b1 + below2 * b2
        for i in range(2):
            cut = slice(i * BROAD, (i + 1) * BROAD)
            field[c, pl.ds(i * PITCH + 8, BROAD), :] = above[cut]
            field[c, pl.ds((10 + i) * PITCH + 8, BROAD), :] = below[cut]
            field[c, pl.ds(i * PITCH + 40, 2), :] = above1[i * BROAD:i * BROAD + 2] * (has_a * has_r)
            field[c, pl.ds((10 + i) * PITCH + 6, 2), :] = below1[i * BROAD + 30:i * BROAD + 32] * (has_b * has_l)

    def land_cols(c, field, k):
        left = cols_r[k, 0, c].astype(F32) * has_l
        right = cols_r[k, 1, c].astype(F32) * has_r
        for i in range(2):
            field[c, pl.ds(2 * PITCH + 6 + i, 8, stride=PITCH), :] = left[i * 8:(i + 1) * 8]
            field[c, pl.ds(2 * PITCH + 40 + i, 8, stride=PITCH), :] = right[i * 8:(i + 1) * 8]

    def convolve(c, field, flipped, put, starts):
        taps = [dwk[c, pl.ds(t, 1), :] for t in range(25)]
        for y in starts:
            acc = [None, None]
            for r in range(6):
                for b in range(5):
                    rows = field[c, pl.ds((y + r) * PITCH + 6 + b, BROAD), :]
                    for k in range(2):
                        a = r - k
                        if 0 <= a < 5:
                            t = 24 - (5 * a + b) if flipped else 5 * a + b
                            term = rows * taps[t]
                            acc[k] = term if acc[k] is None else acc[k] + term
            for k in range(2):
                put(c, y + k, acc[k])

    def post_state(e, j, state, key_sum):
        if STATE_DT == F32:
            tail = jnp.broadcast_to(key_sum, (8, LANES))
        else:
            row = lax.broadcasted_iota(jnp.int32, (8, LANES), 0)
            high = key_sum.astype(BF16).astype(F32)
            tail = jnp.where(row == 0, high, jnp.where(row == 1, key_sum - high, 0.0))
        for r in range(4):
            st_send[e, 4 * j + r] = jnp.concatenate([state[8 * r:8 * r + 8], tail], axis=0).astype(STATE_DT)

    def rs(e, d):
        p = peer(d)
        return push(st_send.at[e, p], st_recv.at[e, me], rs_s.at[e, d], rs_r.at[e, me], {"tile": p})

    def rs_from(e, d):
        p = peer(d)
        return push(st_send.at[e, p], st_recv.at[e, p], rs_s.at[e, d], rs_r.at[e, p], {"tile": p})

    def ag(e, d):
        p = peer(d)
        return push(st_tot.at[e, p], st_out.at[e, me], ag_s.at[e, d], ag_r.at[e, me], {"tile": p})

    def ag_from(e, d):
        p = peer(d)
        return push(st_tot.at[e, p], st_out.at[e, p], ag_s.at[e, d], ag_r.at[e, p], {"tile": p})

    def scatter(e):
        loop(1, TILES, lambda d: rs(e, d).start())
        st_recv[e, me] = st_send[e, me]

    def total(e):
        loop(1, TILES, lambda d: rs_from(e, d).wait_recv())
        run = st_recv[e, 0].astype(F32)
        runs = [run]
        for s in range(1, TILES):
            run = run * keep[s] + st_recv[e, s].astype(F32)
            runs.append(run)
        for s in range(TILES - 1, -1, -1):
            if s < TILES - 1:
                run = run * keep[s + 1] + runs[s] * (one - keep[s + 1])
            if STATE_DT == F32:
                st_tot[e, s] = run
            else:
                row = lax.broadcasted_iota(jnp.int32, (8, LANES), 0)
                key_sum = run[8:9] + run[9:10]
                high = key_sum.astype(BF16).astype(F32)
                tail = jnp.where(row == 0, high, jnp.where(row == 1, key_sum - high, 0.0))
                st_tot[e, s] = jnp.concatenate([run[0:8], tail], axis=0).astype(STATE_DT)
        loop(1, TILES, lambda d: ag(e, d).start())
        st_out[e, me] = st_tot[e, me]

    def gather(e):
        loop(1, TILES, lambda d: ag_from(e, d).wait_recv())

    def get_state(e, j):
        parts = [st_out[e, 4 * j + r].astype(F32) for r in range(4)]
        state = expand(jnp.concatenate([part[0:8] for part in parts], axis=0))
        key_sum = parts[0][8:9]
        if STATE_DT != F32:
            key_sum = key_sum + parts[0][9:10]
        return (split(state) if STATE_DT == F32 else (state.astype(BF16),)), key_sum

    def terms(scale, j):
        if scale == 0:
            raw = x_live[j]
            return raw.astype(F32), (raw,)
        raw = mrg[j]
        return raw, split(raw)

    def relu_terms(scale, j):
        raw, parts = terms(scale, j)
        rect = jnp.maximum(raw, 0.0)
        return raw, rect, ((rect.astype(BF16),) if scale == 0 else split(rect))

    def states(scale):
        def body(j):
            _, rect, keys = relu_terms(scale, 4 + j)
            _, values = terms(scale, 8 + j)
            post_state(scale, j, compact(mm(keys, values, TN)), jnp.sum(rect, axis=0, keepdims=True))
        loop(0, 4, body)

    def attend(scale, grads):
        def body(j):
            state, key_sum = get_state(scale, j)
            raw, rect, queries = relu_terms(scale, j)
            den = mm(split(rect * key_sum), same_bf, NN) + EPSILON
            inverse = 1.0 / den
            num = mm(queries, state, NN)
            grad = c_in[4 * scale + j].astype(F32)
            grad_num = grad * inverse
            grad_den = -mm(split(grad_num * num), same_bf, NN) * inverse
            grad_parts = split(grad_num)
            grad_query = mm(grad_parts, state, NT) + grad_den * key_sum
            grads[j] = jnp.where(raw > 0, grad_query, 0.0)
            post_state(2 + scale, j, compact(mm(queries, grad_parts, TN)),
                       jnp.sum(rect * grad_den, axis=0, keepdims=True))
        loop(0, 4, body)

    def attend_back(scale, grads):
        def body(j):
            state, key_sum = get_state(2 + scale, j)
            raw, _, keys = relu_terms(scale, 4 + j)
            _, values = terms(scale, 8 + j)
            grad_key = mm(values, state, NT) + key_sum
            grads[4 + j] = jnp.where(raw > 0, grad_key, 0.0)
            grads[8 + j] = mm(keys, state, NN)
        loop(0, 4, body)

    loop(0, NB, lambda c: stage(c, pad, 0))
    stage_corners(pad, 0, 0, NB)
    states(0)
    pl.semaphore_wait(barrier, (TILES - 1) + (nx - 1) + (ny - 1))
    halo_kv, halo_q = halo(0, QB, NB), halo(0, 0, QB)
    for copy in halo_kv:
        copy.start()
    scatter(0)
    for copy in halo_q:
        copy.start()
    for c in range(NB):
        lanes = pl.ds(c * LANES, LANES)
        pltpu.make_async_copy(dw.at[:, lanes], dwk.at[c], in_sem.at[NB + c]).wait()
        pltpu.make_async_copy(pw.at[:, lanes], pwk.at[c], in_sem.at[2 * NB + c]).wait()
    for c in range(8):
        pltpu.make_async_copy(cot.at[:, pl.ds(c * LANES, LANES)], c_in.at[c], in_sem.at[3 * NB + c]).wait()

    def put_mix(c, y, rows):
        mix[c, y * BROAD:(y + 1) * BROAD, :] = rows

    def inner(c):
        land_cols(c, pad, 0)
        convolve(c, pad, False, put_mix, (2, 4))

    def outer(c):
        land_rows(c, pad, 0)
        convolve(c, pad, False, put_mix, (0, 6))
        weight = split(expand(pwk[c]))
        mrg[c] = mm(split(mix[c]), weight, NN)

    for copy in halo_kv[:4]:
        copy.wait_recv()
    land_corners(pad, 0, QB, NB)
    loop(QB, NB, inner)
    for copy in halo_kv[4:]:
        copy.wait_recv()
    loop(QB, NB, outer)
    states(1)
    scatter(1)
    total(0)
    for copy in halo_q:
        copy.wait_recv()
    land_corners(pad, 0, 0, QB)
    loop(0, QB, lambda c: (inner(c), outer(c)))
    total(1)
    gather(0)
    attend(0, gsrc)
    scatter(2)
    gather(1)
    attend(1, gmrg)
    scatter(3)
    total(2)

    dw_tmp[...] = jnp.zeros((32, LANES), F32)

    def backward(c):
        weight = split(expand(pwk[c]))
        grads = split(gmrg[c] * live)
        grad_mix = mm(grads, weight, NT)
        for y in range(TALL):
            pad2[c, pl.ds((2 + y) * PITCH + 8, BROAD), :] = grad_mix[y * BROAD:(y + 1) * BROAD]
        rows_s[0, c] = grad_mix[POS - 64:].astype(BF16)
        rows_s[1, c] = grad_mix[:64].astype(BF16)
        stage(c, pad2, 1)
        grad_pw = compact(mm(split(mix[c]), grads, TN))
        for b in range(5):
            acc = [None] * 5
            for r in range(12):
                rows = pad[c, pl.ds(r * PITCH + 6 + b, BROAD), :]
                for a in range(5):
                    y = r - a
                    if 0 <= y < TALL:
                        term = rows * pad2[c, pl.ds((2 + y) * PITCH + 8, BROAD), :]
                        acc[a] = term if acc[a] is None else acc[a] + term
            for a in range(5):
                t = 5 * a + b
                dw_tmp[t:t + 1, :] = jnp.sum(acc[a], axis=0, keepdims=True)
        for i in range(2):
            g_send[4 * c + i] = grad_pw[16 * i:16 * i + 16].astype(GRAD_DT)
            g_send[4 * c + 2 + i] = dw_tmp[16 * i:16 * i + 16, :].astype(GRAD_DT)

    def add_up(ref, count, lo, n):
        acc = ref[0, lo:lo + n].astype(F32)
        for s in range(1, count):
            acc = acc + ref[s, lo:lo + n].astype(F32)
        return acc

    class Part:
        def __init__(self, k, first, lo, n):
            self.k, self.first, self.lo, self.n = k, first, lo, n
            self.cut = pl.ds(lo, n)

        def piece(self, p):
            return pl.ds(self.first + self.n * p, self.n)

        def rs(self, d, slot_of):
            p = peer(d)
            return push(g_send.at[self.piece(p)], g_recv.at[slot_of, self.cut],
                        gr_s.at[self.k, d], gr_r.at[self.k, slot_of], {"tile": p})

        def x(self, d, slot_of):
            return push(g_x.at[mx, self.cut], g_x.at[slot_of, self.cut],
                        gx_s.at[self.k, d], gx_r.at[self.k, slot_of], {"img": x_peer(d)})

        def y(self, d, slot_of):
            return push(g_y.at[my, self.cut], g_y.at[slot_of, self.cut],
                        gy_s.at[self.k, d], gy_r.at[self.k, slot_of], {"img": y_peer(d)})

        def ag(self, d, slot_of):
            return push(g_tot.at[self.cut], g_all.at[self.piece(slot_of)],
                        ga_s.at[self.k, d], ga_r.at[self.k, slot_of], {"tile": peer(d)})

        def scatter(self):
            loop(1, TILES, lambda d: self.rs(d, me).start())
            g_recv[me, self.lo:self.lo + self.n] = g_send[self.piece(me)]

        def send_x(self):
            loop(1, TILES, lambda d: self.rs(d, peer(d)).wait_recv())
            g_x[mx, self.lo:self.lo + self.n] = add_up(g_recv, TILES, self.lo, self.n)
            if nx > 1:
                loop(1, nx, lambda d: self.x(d, mx).start())

        def send_y(self):
            if nx > 1:
                loop(1, nx, lambda d: self.x(d, (mx + d) % nx).wait_recv())
            g_y[my, self.lo:self.lo + self.n] = add_up(g_x, nx, self.lo, self.n)
            if ny > 1:
                loop(1, ny, lambda d: self.y(d, my).start())

        def send_all(self):
            if ny > 1:
                loop(1, ny, lambda d: self.y(d, (my + d) % ny).wait_recv())
            g_tot[self.lo:self.lo + self.n] = (add_up(g_y, ny, self.lo, self.n) * norm).astype(GRAD_DT)
            loop(1, TILES, lambda d: self.ag(d, me).start())
            g_all[self.piece(me)] = g_tot[self.lo:self.lo + self.n]

        def finish(self):
            loop(1, TILES, lambda d: self.ag(d, peer(d)).wait_recv())

        def drain(self):
            def body(d):
                self.rs(d, me).wait_send()
                self.ag(d, me).wait_send()
            loop(1, TILES, body)
            if nx > 1:
                loop(1, nx, lambda d: self.x(d, mx).wait_send())
            if ny > 1:
                loop(1, ny, lambda d: self.y(d, my).wait_send())

    part_q, part_kv = Part(0, 0, 0, 1), Part(1, 16, 1, 2)

    def put_out(c, y, rows):
        rows = (rows + gsrc[c, y * BROAD:(y + 1) * BROAD, :]) * live
        o_blk[c, y * BROAD:(y + 1) * BROAD, :] = rows.astype(BF16)

    def out_copy(c):
        lanes = pl.ds(pl.multiple_of(c * LANES, LANES), LANES)
        return pltpu.make_async_copy(o_blk.at[c], out.at[:, lanes], out_sem.at[c])

    def last(c):
        land_cols(c, pad2, 1)
        land_rows(c, pad2, 1)
        convolve(c, pad2, True, put_out, (0, 2, 4, 6))
        out_copy(c).start()

    loop(0, QB, backward)
    part_q.scatter()
    stage_corners(pad2, 1, 0, QB)
    back_q = halo(1, 0, QB)
    for copy in back_q:
        copy.start()
    total(3)
    gather(2)
    attend_back(0, gsrc)
    part_q.send_x()
    for copy in back_q:
        copy.wait_recv()
    land_corners(pad2, 1, 0, QB)
    loop(0, QB, last)
    gather(3)
    attend_back(1, gmrg)
    part_q.send_y()
    loop(QB, NB, backward)
    part_kv.scatter()
    stage_corners(pad2, 1, QB, NB)
    back_kv = halo(1, QB, NB)
    for copy in back_kv:
        copy.start()
    part_q.send_all()
    part_kv.send_x()
    for copy in back_kv:
        copy.wait_recv()
    land_corners(pad2, 1, QB, NB)
    loop(QB, QB + 3, last)
    part_kv.send_y()
    loop(QB + 3, NB, last)
    part_kv.send_all()

    for copy in halo_kv + halo_q + back_q + back_kv:
        copy.wait_send()

    def drain(d):
        for e in range(4):
            rs(e, d).wait_send()
            ag(e, d).wait_send()

    loop(1, TILES, drain)
    loop(0, NB, lambda c: out_copy(c).wait())
    part_q.finish()
    part_kv.finish()
    part_q.drain()
    part_kv.drain()
    g_fin[...] = g_all[...]


def write(grad, sums, out, gdw, gpw, rows, in_sem, out_sem):
    steps = 4
    size = POS // steps

    def take(i):
        return pltpu.make_async_copy(grad.at[pl.ds(i * size, size)], rows.at[pl.ds(i * size, size)], in_sem.at[i])

    def give(i):
        return pltpu.make_async_copy(rows.at[pl.ds(i * size, size)], out.at[pl.ds(i * size, size)], out_sem.at[i])

    for i in range(steps):
        take(i).start()
    for c in range(NB):
        lanes = slice(c * LANES, (c + 1) * LANES)
        for i in range(2):
            gpw[16 * i:16 * i + 16, lanes] = sums[4 * c + i].astype(F32)
        gdw[0:16, lanes] = sums[4 * c + 2].astype(F32)
        gdw[16:25, lanes] = sums[4 * c + 3].astype(F32)[0:9]
    for i in range(steps):
        take(i).wait()
        give(i).start()
    for i in range(steps):
        give(i).wait()


def local(nx, ny, qkv, cotangent, dw_weight, pw_weight, tile_image, tile_row, tile_col, image_height, image_width):
    channels, inner = qkv.shape[4], cotangent.shape[4]
    norm = 1.0 / math.sqrt(POS * lax.axis_size("tile") * lax.axis_size("img"))
    dma = pltpu.SemaphoreType.DMA
    vm = pltpu.VMEM
    any_spec = pl.BlockSpec(memory_space=pl.ANY)
    smem = pl.BlockSpec(memory_space=pltpu.SMEM)
    vmem = pl.BlockSpec(memory_space=pltpu.VMEM)
    scratch = [
        vm((NB, POS, LANES), BF16), vm((NB, POS, LANES), BF16), vm((8, POS, LANES), BF16),
        vm((NB, 25, LANES), F32), vm((NB, HD, LANES), F32),
        vm((NB, 12 * PITCH, LANES), F32), vm((NB, 12 * PITCH, LANES), F32),
        vm((NB, POS, LANES), F32), vm((NB, POS, LANES), F32), vm((NB, POS, LANES), F32), vm((NB, POS, LANES), F32),
        vm((NB, POS, LANES), BF16),
        vm((4, TILES, 16, LANES), STATE_DT), vm((4, TILES, 16, LANES), STATE_DT),
        vm((4, TILES, 16, LANES), STATE_DT), vm((4, TILES, 16, LANES), STATE_DT),
        vm((16, LANES), F32), vm((48, LANES), F32),
        vm((2, 2, NB, 16, LANES), BF16), vm((2, 2, 48, LANES), BF16), vm((2, NB, 64, LANES), BF16),
        vm((2, 4, NB, 64, LANES), BF16), vm((2, 2, NB, 16, LANES), BF16), vm((2, 2, 48, LANES), BF16),
        vm((32, LANES), F32),
        vm((48, 16, LANES), GRAD_DT), vm((TILES, 3, 16, LANES), GRAD_DT),
        vm((nx, 3, 16, LANES), F32), vm((ny, 3, 16, LANES), F32),
        vm((3, 16, LANES), GRAD_DT), vm((48, 16, LANES), GRAD_DT),
        dma((3 * NB + 8,)), dma((NB,)),
        dma((4, TILES)), dma((4, TILES)), dma((4, TILES)), dma((4, TILES)),
        dma((2, 2, 8)), dma((2, 2, 8)),
        dma((2, TILES)), dma((2, TILES)), dma((2, nx)), dma((2, nx)), dma((2, ny)), dma((2, ny)),
        dma((2, TILES)), dma((2, TILES)),
    ]
    grad, sums = pl.pallas_call(
        functools.partial(kernel, nx, ny, norm),
        out_shape=(jax.ShapeDtypeStruct((POS, channels), BF16), jax.ShapeDtypeStruct((4 * NB, 16, LANES), GRAD_DT)),
        in_specs=[any_spec] * 4 + [smem] * 5,
        out_specs=(any_spec, vmem),
        scratch_shapes=scratch,
        compiler_params=pltpu.CompilerParams(
            collective_id=0, has_side_effects=True, vmem_limit_bytes=60 * 1024 * 1024
        ),
        name="linear_attention",
    )(
        qkv.reshape(POS, channels), cotangent.reshape(POS, inner), dw_weight, pw_weight,
        tile_image, tile_row, tile_col, image_height, image_width,
    )
    grad, grad_dw, grad_pw = pl.pallas_call(
        write,
        out_shape=(
            jax.ShapeDtypeStruct((POS, channels), BF16),
            jax.ShapeDtypeStruct((25, channels), F32),
            jax.ShapeDtypeStruct((HD, channels), F32),
        ),
        in_specs=[any_spec, vmem],
        out_specs=(any_spec, vmem, vmem),
        scratch_shapes=[vm((POS, channels), BF16), dma((4,)), dma((4,))],
        name="write_outputs",
    )(grad, sums)
    return grad.reshape(qkv.shape), grad_dw, grad_pw


def solution(mesh):
    placed = (
        P("img", "tile", None, None, None),
        P("img", "tile", None, None, None),
        P(),
        P(),
        P("img", "tile"),
        P("img", "tile"),
        P("img", "tile"),
        P("img", None),
        P("img", None),
    )
    count = mesh.shape["img"]
    nx = {32: 4, 4: 2}.get(count, 1)
    return jax.shard_map(
        functools.partial(local, nx, count // nx),
        mesh=mesh,
        in_specs=placed,
        out_specs=(P("img", "tile", None, None, None), P(), P()),
        check_vma=False,
    )
```

```python
import functools
import math

import jax
import jax.numpy as jnp
from jax import lax
from jax.experimental import pallas as pl
from jax.experimental.pallas import tpu as pltpu
from jax.sharding import PartitionSpec as P

MESH = pl.DeviceIdType.MESH
F32, BF16 = jnp.float32, jnp.bfloat16
EPSILON = 1e-06
TALL, BROAD, LANES, HD = 8, 32, 128, 32
POS = TALL * BROAD
PITCH = 48
NB = 12
TILES = 16
STATE_DT = BF16
GRAD_DT = BF16
QB = 4


def split(x):
    hi = x.astype(BF16)
    return hi, (x - hi.astype(F32)).astype(BF16)


def dot(a, b, dims):
    return lax.dot_general(a, b, (dims, ((), ())), preferred_element_type=F32)


NN, NT, TN = ((1,), (0,)), ((1,), (1,)), ((0,), (0,))


def mm(a, b, dims):
    out = dot(a[0], b[0], dims)
    if len(b) > 1:
        out = out + dot(a[0], b[1], dims)
    if len(a) > 1:
        out = out + dot(a[1], b[0], dims)
    return out


def kernel(nx, ny, norm, qkv, cot, dw, pw, im_h_in, im_w_in, out, g_fin, *scratch):
    (x_raw, c_in, dwk, pwk, pad, pad2, mix, mrg, gsrc, gmrg, im_h, im_w,
     st_send, st_recv, st_tot, st_out,
     cols_f, corner_f, cols_s, corner_s, rows_s, rows_r, cols_r, corner_r,
     dw_tmp, g_send, g_recv, g_x, g_y, g_tot, g_all,
     in_sem, meta_sem, rs_s, rs_r, ag_s, ag_r, h_s, h_r, gr_s, gr_r, gx_s, gx_r, gy_s, gy_r, ga_s, ga_r) = scratch
    me = lax.axis_index("tile")
    im = lax.axis_index("img")
    mx, my = im // ny, im % ny

    def peer(d):
        return (me + d + TILES) % TILES

    def x_peer(d):
        return ((mx + d) % nx) * ny + my

    def y_peer(d):
        return mx * ny + (my + d) % ny

    def push(src, dst, ssem, rsem, where):
        return pltpu.make_async_remote_copy(
            src_ref=src, dst_ref=dst, send_sem=ssem, recv_sem=rsem, device_id=where, device_id_type=MESH
        )

    def loop(lo, hi, body):
        lax.fori_loop(lo, hi, lambda i, carry: (body(i), carry)[1], 0)

    def far_first(count, body):
        loop(0, count - 1, lambda i: body(count // 2 + ((i + 1) // 2) * (1 - 2 * (i % 2))))

    def in_copies():
        copies = []
        for c in range(NB):
            lanes = pl.ds(c * LANES, LANES)
            copies.append(pltpu.make_async_copy(qkv.at[:, lanes], x_raw.at[c], in_sem.at[c]))
            copies.append(pltpu.make_async_copy(dw.at[:, lanes], dwk.at[c], in_sem.at[NB + c]))
            copies.append(pltpu.make_async_copy(pw.at[:, lanes], pwk.at[c], in_sem.at[2 * NB + c]))
        for c in range(8):
            lanes = pl.ds(c * LANES, LANES)
            copies.append(pltpu.make_async_copy(cot.at[:, lanes], c_in.at[c], in_sem.at[3 * NB + c]))
        return copies

    meta = [
        pltpu.make_async_copy(src, dst, meta_sem.at[i])
        for i, (src, dst) in enumerate(
            ((im_h_in, im_h), (im_w_in, im_w)))
    ]
    for copy in meta + in_copies():
        copy.start()

    barrier = pltpu.get_barrier_semaphore()
    far_first(TILES, lambda d: pl.semaphore_signal(
        barrier, inc=1, device_id={"tile": peer(d)}, device_id_type=MESH))
    if nx > 1:
        far_first(nx, lambda d: pl.semaphore_signal(
            barrier, inc=1, device_id={"img": x_peer(d)}, device_id_type=MESH))
    if ny > 1:
        far_first(ny, lambda d: pl.semaphore_signal(
            barrier, inc=1, device_id={"img": y_peer(d)}, device_id_type=MESH))

    one, zero = jnp.float32(1), jnp.float32(0)

    def flag(cond):
        return jnp.where(cond, one, zero)

    lane_head = lax.broadcasted_iota(jnp.int32, (LANES, LANES), 1) // HD
    row_head = lax.broadcasted_iota(jnp.int32, (LANES, LANES), 0) // HD
    same_head = flag(lane_head == row_head)
    same_bf = (same_head.astype(BF16),)

    def expand(compact):
        return jnp.concatenate([compact] * 4, axis=0) * same_head

    def compact(full):
        masked = full * same_head
        return masked[0:32] + masked[32:64] + masked[64:96] + masked[96:128]

    def place(c):
        pltpu.make_async_copy(qkv.at[:, pl.ds(0, LANES)], x_raw.at[c], in_sem.at[c]).wait()
        for y in range(TALL):
            rows = x_raw[c, y * BROAD:(y + 1) * BROAD, :].astype(F32)
            pad[c, pl.ds((2 + y) * PITCH + 8, BROAD), :] = rows

    loop(0, NB, place)

    def stage(c, field, k):
        for side, first in ((0, 38), (1, 8)):
            for i in range(2):
                cols_f[i * 8:(i + 1) * 8, :] = field[c, pl.ds(2 * PITCH + first + i, 8, stride=PITCH), :]
            cols_s[k, side, c] = cols_f[...].astype(BF16)

    def stage_corners(field, k, lo, hi):
        for side, row, first in ((0, 8, 38), (1, 2, 8)):
            for c in range(lo, hi):
                for i in range(2):
                    corner_f[4 * c + 2 * i:4 * c + 2 * i + 2, :] = field[c, pl.ds((row + i) * PITCH + first, 2), :]
            corner_s[k, side, 4 * lo:4 * hi] = corner_f[4 * lo:4 * hi, :].astype(BF16)

    def halo(k, lo, hi):
        blocks, group = pl.ds(lo, hi - lo), lo // QB
        corner = pl.ds(4 * lo, 4 * (hi - lo))
        if k == 0:
            bottom, top = x_raw.at[blocks, pl.ds(POS - 64, 64)], x_raw.at[blocks, pl.ds(0, 64)]
        else:
            bottom, top = rows_s.at[0, blocks], rows_s.at[1, blocks]
        plan = [
            (cols_s.at[k, 0, blocks], cols_r.at[k, 0, blocks], 1), (cols_s.at[k, 1, blocks], cols_r.at[k, 1, blocks], -1),
            (corner_s.at[k, 0, corner], corner_r.at[k, 0, corner], 3),
            (corner_s.at[k, 1, corner], corner_r.at[k, 1, corner], -3),
            (bottom, rows_r.at[k, 2, blocks], 2), (top, rows_r.at[k, 3, blocks], -2),
            (bottom, rows_r.at[k, 0, blocks], 1), (top, rows_r.at[k, 1, blocks], -1),
        ]
        return [
            push(src, dst, h_s.at[k, group, i], h_r.at[k, group, i], {"tile": peer(step)})
            for i, (src, dst, step) in enumerate(plan)
        ]

    def land_corners(field, k, lo, hi):
        for side, row, first, has in ((0, 0, 6, has_a * has_l), (1, 10, 40, has_b * has_r)):
            corner_f[4 * lo:4 * hi, :] = corner_r[k, side, 4 * lo:4 * hi].astype(F32) * has
            for c in range(lo, hi):
                for i in range(2):
                    field[c, pl.ds((row + i) * PITCH + first, 2), :] = corner_f[4 * c + 2 * i:4 * c + 2 * i + 2, :]

    def land_rows(c, field, k):
        above1, below1 = rows_r[k, 0, c].astype(F32), rows_r[k, 1, c].astype(F32)
        above2, below2 = rows_r[k, 2, c].astype(F32), rows_r[k, 3, c].astype(F32)
        above = above1 * a1 + above2 * a2
        below = below1 * b1 + below2 * b2
        for i in range(2):
            cut = slice(i * BROAD, (i + 1) * BROAD)
            field[c, pl.ds(i * PITCH + 8, BROAD), :] = above[cut]
            field[c, pl.ds((10 + i) * PITCH + 8, BROAD), :] = below[cut]
            field[c, pl.ds(i * PITCH + 40, 2), :] = above1[i * BROAD:i * BROAD + 2] * (has_a * has_r)
            field[c, pl.ds((10 + i) * PITCH + 6, 2), :] = below1[i * BROAD + 30:i * BROAD + 32] * (has_b * has_l)

    def land_cols(c, field, k):
        left = cols_r[k, 0, c].astype(F32) * has_l
        right = cols_r[k, 1, c].astype(F32) * has_r
        for i in range(2):
            field[c, pl.ds(2 * PITCH + 6 + i, 8, stride=PITCH), :] = left[i * 8:(i + 1) * 8]
            field[c, pl.ds(2 * PITCH + 40 + i, 8, stride=PITCH), :] = right[i * 8:(i + 1) * 8]

    def convolve(c, field, flipped, put, starts):
        taps = [dwk[c, pl.ds(t, 1), :] for t in range(25)]
        for y in starts:
            acc = [None, None]
            for r in range(6):
                for b in range(5):
                    rows = field[c, pl.ds((y + r) * PITCH + 6 + b, BROAD), :]
                    for k in range(2):
                        a = r - k
                        if 0 <= a < 5:
                            t = 24 - (5 * a + b) if flipped else 5 * a + b
                            term = rows * taps[t]
                            acc[k] = term if acc[k] is None else acc[k] + term
            for k in range(2):
                put(c, y + k, acc[k])

    def post_state(e, j, state, key_sum):
        if STATE_DT == F32:
            tail = jnp.broadcast_to(key_sum, (8, LANES))
        else:
            row = lax.broadcasted_iota(jnp.int32, (8, LANES), 0)
            high = key_sum.astype(BF16).astype(F32)
            tail = jnp.where(row == 0, high, jnp.where(row == 1, key_sum - high, 0.0))
        for r in range(4):
            st_send[e, 4 * j + r] = jnp.concatenate([state[8 * r:8 * r + 8], tail], axis=0).astype(STATE_DT)

    def rs(e, d):
        p = peer(d)
        return push(st_send.at[e, p], st_recv.at[e, me], rs_s.at[e, d], rs_r.at[e, me], {"tile": p})

    def rs_from(e, d):
        p = peer(d)
        return push(st_send.at[e, p], st_recv.at[e, p], rs_s.at[e, d], rs_r.at[e, p], {"tile": p})

    def ag(e, d):
        p = peer(d)
        return push(st_tot.at[e, p], st_out.at[e, me], ag_s.at[e, d], ag_r.at[e, me], {"tile": p})

    def ag_from(e, d):
        p = peer(d)
        return push(st_tot.at[e, p], st_out.at[e, p], ag_s.at[e, d], ag_r.at[e, p], {"tile": p})

    def scatter(e):
        far_first(TILES, lambda d: rs(e, d).start())
        st_recv[e, me] = st_send[e, me]

    def total(e):
        loop(1, TILES, lambda d: rs_from(e, d).wait_recv())
        part = [st_recv[e, s].astype(F32) for s in range(TILES)]
        ahead, behind = [part[0]], [jnp.zeros_like(part[0])]
        for s in range(1, TILES):
            ahead.append(ahead[-1] * keep[s] + part[s])
            behind.append((behind[-1] + part[TILES - s]) * keep[TILES - s])
        for s in range(TILES):
            run = ahead[s] + behind[TILES - 1 - s]
            if STATE_DT == F32:
                st_tot[e, s] = run
            else:
                row = lax.broadcasted_iota(jnp.int32, (8, LANES), 0)
                key_sum = run[8:9] + run[9:10]
                high = key_sum.astype(BF16).astype(F32)
                tail = jnp.where(row == 0, high, jnp.where(row == 1, key_sum - high, 0.0))
                st_tot[e, s] = jnp.concatenate([run[0:8], tail], axis=0).astype(STATE_DT)
        far_first(TILES, lambda d: ag(e, d).start())
        st_out[e, me] = st_tot[e, me]

    def gather(e):
        loop(1, TILES, lambda d: ag_from(e, d).wait_recv())

    def get_state(e, j):
        parts = [st_out[e, 4 * j + r].astype(F32) for r in range(4)]
        state = expand(jnp.concatenate([part[0:8] for part in parts], axis=0))
        key_sum = parts[0][8:9]
        if STATE_DT != F32:
            key_sum = key_sum + parts[0][9:10]
        return (split(state) if STATE_DT == F32 else (state.astype(BF16),)), key_sum

    def terms(scale, j):
        if scale == 0:
            raw = x_raw[j]
            return raw.astype(F32), (raw,)
        raw = mrg[j]
        return raw, split(raw)

    def relu_terms(scale, j):
        raw, parts = terms(scale, j)
        rect = jnp.maximum(raw, 0.0)
        return raw, rect, ((rect.astype(BF16),) if scale == 0 else split(rect))

    def states(scale):
        def body(j):
            _, rect, keys = relu_terms(scale, 4 + j)
            _, values = terms(scale, 8 + j)
            post_state(scale, j, compact(mm(keys, values, TN)), jnp.sum(rect, axis=0, keepdims=True))
        loop(0, 4, body)

    def attend(scale, grads):
        def body(j):
            state, key_sum = get_state(scale, j)
            raw, rect, queries = relu_terms(scale, j)
            den = mm(split(rect * key_sum), same_bf, NN) + EPSILON
            inverse = 1.0 / den
            num = mm(queries, state, NN)
            grad = c_in[4 * scale + j].astype(F32)
            grad_num = grad * inverse
            grad_den = -mm(split(grad_num * num), same_bf, NN) * inverse
            grad_parts = split(grad_num)
            grad_query = mm(grad_parts, state, NT) + grad_den * key_sum
            grads[j] = jnp.where(raw > 0, grad_query, 0.0)
            post_state(2 + scale, j, compact(mm(queries, grad_parts, TN)),
                       jnp.sum(rect * grad_den, axis=0, keepdims=True))
        loop(0, 4, body)

    def attend_back(scale, grads):
        def body(j):
            state, key_sum = get_state(2 + scale, j)
            raw, _, keys = relu_terms(scale, 4 + j)
            _, values = terms(scale, 8 + j)
            grad_key = mm(values, state, NT) + key_sum
            grads[4 + j] = jnp.where(raw > 0, grad_key, 0.0)
            grads[8 + j] = mm(keys, state, NN)
        loop(0, 4, body)

    loop(0, NB, lambda c: stage(c, pad, 0))
    stage_corners(pad, 0, 0, NB)
    pl.semaphore_wait(barrier, (TILES - 1) + (nx - 1) + (ny - 1))
    halo_q, halo_k, halo_v = (halo(0, lo, lo + QB) for lo in (0, QB, 2 * QB))
    for copy in halo_k[:4] + halo_v[:4] + halo_k[4:] + halo_v[4:]:
        copy.start()
    states(0)
    scatter(0)
    for copy in halo_q:
        copy.start()

    for copy in meta:
        copy.wait()
    slots = im_h.shape[1]
    tall, wide, first, end = (jnp.int32(0) for _ in range(4))
    ends = []
    for m in range(slots):
        start = end
        end = end + im_h[0, m] * im_w[0, m]
        mine = (start <= me) & (me < end)
        tall = tall + jnp.where(mine, im_h[0, m], 0)
        wide = wide + jnp.where(mine, im_w[0, m], 0)
        first = first + jnp.where(mine, start, 0)
        ends.append(end)
    live = flag(me < end)
    within = me - first
    col = jnp.where(wide == 2, within % 2, 0)
    row = jnp.where(wide == 2, within // 2, within)
    has_l = live * flag(col > 0)
    has_r = live * flag(col < wide - 1)
    has_a = live * flag(row > 0)
    has_b = live * flag(row < tall - 1)
    thin = flag(wide == 1)
    a1, a2, b1, b2 = has_a * thin, has_a * (one - thin), has_b * thin, has_b * (one - thin)
    keep = [zero] * TILES
    for s in range(1, TILES):
        joined = one
        for m in range(slots):
            joined = joined * flag(ends[m] != s)
        keep[s] = joined

    for c in range(NB):
        lanes = pl.ds(c * LANES, LANES)
        pltpu.make_async_copy(dw.at[:, lanes], dwk.at[c], in_sem.at[NB + c]).wait()
        pltpu.make_async_copy(pw.at[:, lanes], pwk.at[c], in_sem.at[2 * NB + c]).wait()
    for c in range(8):
        pltpu.make_async_copy(cot.at[:, pl.ds(c * LANES, LANES)], c_in.at[c], in_sem.at[3 * NB + c]).wait()

    def put_mix(c, y, rows):
        mix[c, y * BROAD:(y + 1) * BROAD, :] = rows

    def inner(c):
        land_cols(c, pad, 0)
        convolve(c, pad, False, put_mix, (2, 4))

    def outer(c):
        land_rows(c, pad, 0)
        convolve(c, pad, False, put_mix, (0, 6))
        weight = split(expand(pwk[c]))
        mrg[c] = mm(split(mix[c]), weight, NN)

    for copy in halo_k[:4] + halo_v[:4]:
        copy.wait_recv()
    land_corners(pad, 0, QB, NB)
    loop(QB, NB, inner)
    for copy in halo_k[4:]:
        copy.wait_recv()
    loop(QB, 2 * QB, outer)
    for copy in halo_v[4:]:
        copy.wait_recv()
    loop(2 * QB, NB, outer)
    states(1)
    scatter(1)
    total(0)
    for copy in halo_q:
        copy.wait_recv()
    land_corners(pad, 0, 0, QB)
    loop(0, QB, lambda c: (inner(c), outer(c)))
    total(1)
    gather(0)
    attend(0, gsrc)
    scatter(2)
    gather(1)
    attend(1, gmrg)
    scatter(3)
    total(2)

    dw_tmp[...] = jnp.zeros((32, LANES), F32)

    def backward(c):
        weight = split(expand(pwk[c]))
        grads = split(gmrg[c] * live)
        grad_mix = mm(grads, weight, NT)
        for y in range(TALL):
            pad2[c, pl.ds((2 + y) * PITCH + 8, BROAD), :] = grad_mix[y * BROAD:(y + 1) * BROAD]
        rows_s[0, c] = grad_mix[POS - 64:].astype(BF16)
        rows_s[1, c] = grad_mix[:64].astype(BF16)
        stage(c, pad2, 1)
        grad_pw = compact(mm(split(mix[c]), grads, TN))
        for b in range(5):
            acc = [None] * 5
            for r in range(12):
                rows = pad[c, pl.ds(r * PITCH + 6 + b, BROAD), :]
                for a in range(5):
                    y = r - a
                    if 0 <= y < TALL:
                        term = rows * pad2[c, pl.ds((2 + y) * PITCH + 8, BROAD), :]
                        term = (term[0:8] + term[8:16]) + (term[16:24] + term[24:32])
                        acc[a] = term if acc[a] is None else acc[a] + term
            for a in range(5):
                t = 5 * a + b
                dw_tmp[t:t + 1, :] = jnp.sum(acc[a], axis=0, keepdims=True)
        for i in range(2):
            g_send[4 * c + i] = grad_pw[16 * i:16 * i + 16].astype(GRAD_DT)
            g_send[4 * c + 2 + i] = dw_tmp[16 * i:16 * i + 16, :].astype(GRAD_DT)

    def add_up(ref, count, lo, n):
        acc = ref[0, lo:lo + n].astype(F32)
        for s in range(1, count):
            acc = acc + ref[s, lo:lo + n].astype(F32)
        return acc

    class Part:
        def __init__(self, k, first, lo, n):
            self.k, self.first, self.lo, self.n = k, first, lo, n
            self.cut = pl.ds(lo, n)

        def piece(self, p):
            return pl.ds(self.first + self.n * p, self.n)

        def rs(self, d, slot_of):
            p = peer(d)
            return push(g_send.at[self.piece(p)], g_recv.at[slot_of, self.cut],
                        gr_s.at[self.k, d], gr_r.at[self.k, slot_of], {"tile": p})

        def x(self, d, slot_of):
            return push(g_x.at[mx, self.cut], g_x.at[slot_of, self.cut],
                        gx_s.at[self.k, d], gx_r.at[self.k, slot_of], {"img": x_peer(d)})

        def y(self, d, slot_of):
            return push(g_y.at[my, self.cut], g_y.at[slot_of, self.cut],
                        gy_s.at[self.k, d], gy_r.at[self.k, slot_of], {"img": y_peer(d)})

        def ag(self, d, slot_of):
            return push(g_tot.at[self.cut], g_all.at[self.piece(slot_of)],
                        ga_s.at[self.k, d], ga_r.at[self.k, slot_of], {"tile": peer(d)})

        def scatter(self):
            far_first(TILES, lambda d: self.rs(d, me).start())
            g_recv[me, self.lo:self.lo + self.n] = g_send[self.piece(me)]

        def send_x(self):
            loop(1, TILES, lambda d: self.rs(d, peer(d)).wait_recv())
            g_x[mx, self.lo:self.lo + self.n] = add_up(g_recv, TILES, self.lo, self.n)
            if nx > 1:
                far_first(nx, lambda d: self.x(d, mx).start())

        def send_y(self):
            if nx > 1:
                loop(1, nx, lambda d: self.x(d, (mx + d) % nx).wait_recv())
            g_y[my, self.lo:self.lo + self.n] = add_up(g_x, nx, self.lo, self.n)
            if ny > 1:
                far_first(ny, lambda d: self.y(d, my).start())

        def send_all(self):
            if ny > 1:
                loop(1, ny, lambda d: self.y(d, (my + d) % ny).wait_recv())
            g_tot[self.lo:self.lo + self.n] = (add_up(g_y, ny, self.lo, self.n) * norm).astype(GRAD_DT)
            far_first(TILES, lambda d: self.ag(d, me).start())
            g_all[self.piece(me)] = g_tot[self.lo:self.lo + self.n]

        def finish(self):
            loop(1, TILES, lambda d: self.ag(d, peer(d)).wait_recv())

        def drain(self):
            def body(d):
                self.rs(d, me).wait_send()
                self.ag(d, me).wait_send()
            loop(1, TILES, body)
            if nx > 1:
                loop(1, nx, lambda d: self.x(d, mx).wait_send())
            if ny > 1:
                loop(1, ny, lambda d: self.y(d, my).wait_send())

    part_q, part_k, part_v = (Part(k, 16 * k, k, 1) for k in range(3))

    def put_out(c, y, rows):
        rows = (rows + gsrc[c, y * BROAD:(y + 1) * BROAD, :]) * live
        lanes = pl.ds(pl.multiple_of(c * LANES, LANES), LANES)
        out[y * BROAD:(y + 1) * BROAD, lanes] = rows.astype(BF16)

    def last(c):
        land_cols(c, pad2, 1)
        land_rows(c, pad2, 1)
        convolve(c, pad2, True, put_out, (0, 2, 4, 6))

    back_q, back_k, back_v = (halo(1, lo, lo + QB) for lo in (0, QB, 2 * QB))

    def send_back(copies, lo):
        stage_corners(pad2, 1, lo, lo + QB)
        for copy in copies:
            copy.start()

    def finish_back(copies, lo):
        for copy in copies:
            copy.wait_recv()
        land_corners(pad2, 1, lo, lo + QB)
        loop(lo, lo + QB, last)

    loop(0, QB, backward)
    part_q.scatter()
    total(3)
    send_back(back_q, 0)
    gather(2)
    attend_back(0, gsrc)
    part_q.send_x()
    gather(3)
    attend_back(1, gmrg)
    part_q.send_y()
    loop(QB, 2 * QB, backward)
    part_k.scatter()
    loop(2 * QB, NB, backward)
    part_v.scatter()
    send_back(back_k, QB)
    send_back(back_v, 2 * QB)
    part_k.send_x()
    part_q.send_all()
    finish_back(back_q, 0)
    part_v.send_x()
    part_k.send_y()
    finish_back(back_k, QB)
    part_v.send_y()
    finish_back(back_v, 2 * QB)
    part_k.send_all()
    part_v.send_all()

    for copy in halo_q + halo_k + halo_v + back_q + back_k + back_v:
        copy.wait_send()

    def drain(d):
        for e in range(4):
            rs(e, d).wait_send()
            ag(e, d).wait_send()

    loop(1, TILES, drain)
    for part in (part_q, part_k, part_v):
        part.finish()
    for part in (part_q, part_k, part_v):
        part.drain()
    g_fin[...] = g_all[...]


def write(grad, sums, out, gdw, gpw, out_sem):
    copy = pltpu.make_async_copy(grad, out, out_sem)
    copy.start()
    for c in range(NB):
        lanes = slice(c * LANES, (c + 1) * LANES)
        for i in range(2):
            gpw[16 * i:16 * i + 16, lanes] = sums[4 * c + i].astype(F32)
        gdw[0:16, lanes] = sums[4 * c + 2].astype(F32)
        gdw[16:25, lanes] = sums[4 * c + 3].astype(F32)[0:9]
    copy.wait()


def local(nx, ny, qkv, cotangent, dw_weight, pw_weight, tile_image, tile_row, tile_col, image_height, image_width):
    channels, inner = qkv.shape[4], cotangent.shape[4]
    norm = 1.0 / math.sqrt(POS * lax.axis_size("tile") * lax.axis_size("img"))
    dma = pltpu.SemaphoreType.DMA
    vm = pltpu.VMEM
    hbm_spec = pl.BlockSpec(memory_space=pltpu.HBM)
    vmem = pl.BlockSpec(memory_space=pltpu.VMEM)
    scratch = [
        vm((NB, POS, LANES), BF16), vm((8, POS, LANES), BF16),
        vm((NB, 25, LANES), F32), vm((NB, HD, LANES), F32),
        vm((NB, 12 * PITCH, LANES), F32), vm((NB, 12 * PITCH, LANES), F32),
        vm((NB, POS, LANES), F32), vm((NB, POS, LANES), F32), vm((NB, POS, LANES), F32), vm((NB, POS, LANES), F32),
        pltpu.SMEM(image_height.shape, jnp.int32), pltpu.SMEM(image_width.shape, jnp.int32),
        vm((4, TILES, 16, LANES), STATE_DT), vm((4, TILES, 16, LANES), STATE_DT),
        vm((4, TILES, 16, LANES), STATE_DT), vm((4, TILES, 16, LANES), STATE_DT),
        vm((16, LANES), F32), vm((48, LANES), F32),
        vm((2, 2, NB, 16, LANES), BF16), vm((2, 2, 48, LANES), BF16), vm((2, NB, 64, LANES), BF16),
        vm((2, 4, NB, 64, LANES), BF16), vm((2, 2, NB, 16, LANES), BF16), vm((2, 2, 48, LANES), BF16),
        vm((32, LANES), F32),
        vm((48, 16, LANES), GRAD_DT), vm((TILES, 3, 16, LANES), GRAD_DT),
        vm((nx, 3, 16, LANES), F32), vm((ny, 3, 16, LANES), F32),
        vm((3, 16, LANES), GRAD_DT), vm((48, 16, LANES), GRAD_DT),
        dma((3 * NB + 8,)), dma((2,)),
        dma((4, TILES)), dma((4, TILES)), dma((4, TILES)), dma((4, TILES)),
        dma((2, 3, 8)), dma((2, 3, 8)),
        dma((3, TILES)), dma((3, TILES)), dma((3, nx)), dma((3, nx)), dma((3, ny)), dma((3, ny)),
        dma((3, TILES)), dma((3, TILES)),
    ]
    grad, sums = pl.pallas_call(
        functools.partial(kernel, nx, ny, norm),
        out_shape=(jax.ShapeDtypeStruct((POS, channels), BF16), jax.ShapeDtypeStruct((4 * NB, 16, LANES), GRAD_DT)),
        in_specs=[hbm_spec] * 6,
        out_specs=(vmem, vmem),
        scratch_shapes=scratch,
        compiler_params=pltpu.CompilerParams(
            collective_id=0, has_side_effects=True, vmem_limit_bytes=40 * 1024 * 1024
        ),
        name="linear_attention",
    )(
        *[pltpu.with_memory_space_constraint(x, pltpu.HBM) for x in (
            qkv.reshape(POS, channels), cotangent.reshape(POS, inner), dw_weight, pw_weight,
            image_height, image_width)]
    )
    grad, grad_dw, grad_pw = pl.pallas_call(
        write,
        out_shape=(
            jax.ShapeDtypeStruct((POS, channels), BF16),
            jax.ShapeDtypeStruct((25, channels), F32),
            jax.ShapeDtypeStruct((HD, channels), F32),
        ),
        in_specs=[vmem, vmem],
        out_specs=(hbm_spec, vmem, vmem),
        scratch_shapes=[dma(())],
        compiler_params=pltpu.CompilerParams(vmem_limit_bytes=8 * 1024 * 1024),
        name="write_outputs",
    )(grad, sums)
    return grad.reshape(qkv.shape), grad_dw, grad_pw


def solution(mesh):
    placed = (
        P("img", "tile", None, None, None),
        P("img", "tile", None, None, None),
        P(),
        P(),
        P("img", "tile"),
        P("img", "tile"),
        P("img", "tile"),
        P("img", None),
        P("img", None),
    )
    count = mesh.shape["img"]
    nx = {32: 4, 4: 2}.get(count, 1)
    return jax.shard_map(
        functools.partial(local, nx, count // nx),
        mesh=mesh,
        in_specs=placed,
        out_specs=(P("img", "tile", None, None, None), P(), P()),
        check_vma=False,
    )
```

```python
import functools
import math

import jax
import jax.numpy as jnp
from jax import lax
from jax.experimental import pallas as pl
from jax.experimental.pallas import tpu as pltpu
from jax.sharding import PartitionSpec as P

MESH = pl.DeviceIdType.MESH
F32, BF16 = jnp.float32, jnp.bfloat16
EPSILON = 1e-06
TALL, BROAD, LANES, HD = 8, 32, 128, 32
POS = TALL * BROAD
PITCH = 48
NB = 12
TILES = 16
STATE_DT = BF16
GRAD_DT = BF16
QB = 4


def split(x):
    hi = x.astype(BF16)
    return hi, (x - hi.astype(F32)).astype(BF16)


def dot(a, b, dims):
    return lax.dot_general(a, b, (dims, ((), ())), preferred_element_type=F32)


NN, NT, TN = ((1,), (0,)), ((1,), (1,)), ((0,), (0,))


def mm(a, b, dims):
    out = dot(a[0], b[0], dims)
    if len(b) > 1:
        out = out + dot(a[0], b[1], dims)
    if len(a) > 1:
        out = out + dot(a[1], b[0], dims)
    return out


def kernel(nx, ny, norm, qkv, cot, dw, pw, im_h_in, im_w_in, out, g_fin, *scratch):
    (x_raw, c_in, m_hi, m_lo, w_hi, w_lo, dwk, pwk, pad, pad2, mix, mrg, gsrc, gmrg, im_h, im_w,
     st_send, st_recv, st_tot, st_out,
     cols_f, corner_f, cols_s, corner_s, rows_s, rows_r, cols_r, corner_r,
     dw_tmp, g_send, g_recv, g_x, g_y, g_tot, g_all,
     in_sem, meta_sem, rs_s, rs_r, ag_s, ag_r, h_s, h_r, gr_s, gr_r, gx_s, gx_r, gy_s, gy_r, ga_s, ga_r) = scratch
    me = lax.axis_index("tile")
    im = lax.axis_index("img")
    mx, my = lax.div(im, ny), lax.rem(im, ny)

    def peer(d):
        return lax.rem(me + (d + TILES), TILES)

    def x_peer(d):
        return lax.rem(mx + d, nx) * ny + my

    def y_peer(d):
        return mx * ny + lax.rem(my + d, ny)

    def push(src, dst, ssem, rsem, where):
        return pltpu.make_async_remote_copy(
            src_ref=src, dst_ref=dst, send_sem=ssem, recv_sem=rsem, device_id=where, device_id_type=MESH
        )

    def loop(lo, hi, body):
        lax.fori_loop(lo, hi, lambda i, carry: (body(i), carry)[1], 0)

    def far_first(count, body):
        half = count // 2
        body(half)
        loop(1, half, lambda h: (body(half - h), body(half + h)))

    def in_copies():
        copies = []
        for c in range(NB):
            lanes = pl.ds(c * LANES, LANES)
            copies.append(pltpu.make_async_copy(qkv.at[:, lanes], x_raw.at[c], in_sem.at[c]))
        for c in range(NB):
            lanes = pl.ds(c * LANES, LANES)
            copies.append(pltpu.make_async_copy(pw.at[:, lanes], pwk.at[c], in_sem.at[2 * NB + c]))
            copies.append(pltpu.make_async_copy(dw.at[:, lanes], dwk.at[c], in_sem.at[NB + c]))
        for c in range(8):
            lanes = pl.ds(c * LANES, LANES)
            copies.append(pltpu.make_async_copy(cot.at[:, lanes], c_in.at[c], in_sem.at[3 * NB + c]))
        return copies

    meta = [
        pltpu.make_async_copy(src, dst, meta_sem.at[i])
        for i, (src, dst) in enumerate(
            ((im_h_in, im_h), (im_w_in, im_w)))
    ]
    for copy in meta + in_copies():
        copy.start()

    barrier = pltpu.get_barrier_semaphore()
    far_first(TILES, lambda d: pl.semaphore_signal(
        barrier, inc=1, device_id={"tile": peer(d)}, device_id_type=MESH))
    if nx > 1:
        far_first(nx, lambda d: pl.semaphore_signal(
            barrier, inc=1, device_id={"img": x_peer(d)}, device_id_type=MESH))
    if ny > 1:
        far_first(ny, lambda d: pl.semaphore_signal(
            barrier, inc=1, device_id={"img": y_peer(d)}, device_id_type=MESH))

    one, zero = jnp.float32(1), jnp.float32(0)

    def flag(cond):
        return jnp.where(cond, one, zero)

    lane_head = lax.broadcasted_iota(jnp.int32, (LANES, LANES), 1) // HD
    row_head = lax.broadcasted_iota(jnp.int32, (LANES, LANES), 0) // HD
    same_head = flag(lane_head == row_head)
    same_bf = (same_head.astype(BF16),)

    def expand(compact):
        return jnp.concatenate([compact] * 4, axis=0) * same_head

    def compact(full):
        masked = full * same_head
        return masked[0:32] + masked[32:64] + masked[64:96] + masked[96:128]

    def place(c):
        pltpu.make_async_copy(qkv.at[:, pl.ds(0, LANES)], x_raw.at[c], in_sem.at[c]).wait()
        for y in range(TALL):
            rows = x_raw[c, y * BROAD:(y + 1) * BROAD, :].astype(F32)
            pad[c, pl.ds((2 + y) * PITCH + 8, BROAD), :] = rows

    loop(0, NB, place)

    def stage(c, field, k):
        for side, first in ((0, 38), (1, 8)):
            for i in range(2):
                cols_f[i * 8:(i + 1) * 8, :] = field[c, pl.ds(2 * PITCH + first + i, 8, stride=PITCH), :]
            cols_s[k, side, c] = cols_f[...].astype(BF16)

    def stage_corners(field, k, lo, hi):
        for side, row, first in ((0, 8, 38), (1, 2, 8)):
            for c in range(lo, hi):
                for i in range(2):
                    corner_f[4 * c + 2 * i:4 * c + 2 * i + 2, :] = field[c, pl.ds((row + i) * PITCH + first, 2), :]
            corner_s[k, side, 4 * lo:4 * hi] = corner_f[4 * lo:4 * hi, :].astype(BF16)

    def halo(k, lo, hi):
        blocks, group = pl.ds(lo, hi - lo), lo // QB
        corner = pl.ds(4 * lo, 4 * (hi - lo))
        if k == 0:
            bottom, top = x_raw.at[blocks, pl.ds(POS - 64, 64)], x_raw.at[blocks, pl.ds(0, 64)]
        else:
            bottom, top = rows_s.at[0, blocks], rows_s.at[1, blocks]
        plan = [
            (cols_s.at[k, 0, blocks], cols_r.at[k, 0, blocks], 1), (cols_s.at[k, 1, blocks], cols_r.at[k, 1, blocks], -1),
            (corner_s.at[k, 0, corner], corner_r.at[k, 0, corner], 3),
            (corner_s.at[k, 1, corner], corner_r.at[k, 1, corner], -3),
            (bottom, rows_r.at[k, 2, blocks], 2), (top, rows_r.at[k, 3, blocks], -2),
            (bottom, rows_r.at[k, 0, blocks], 1), (top, rows_r.at[k, 1, blocks], -1),
        ]
        return [
            push(src, dst, h_s.at[k, group, i], h_r.at[k, group, i], {"tile": peer(step)})
            for i, (src, dst, step) in enumerate(plan)
        ]

    def land_corners(field, k, lo, hi):
        for side, row, first, has in ((0, 0, 6, has_a * has_l), (1, 10, 40, has_b * has_r)):
            corner_f[4 * lo:4 * hi, :] = corner_r[k, side, 4 * lo:4 * hi].astype(F32) * has
            for c in range(lo, hi):
                for i in range(2):
                    field[c, pl.ds((row + i) * PITCH + first, 2), :] = corner_f[4 * c + 2 * i:4 * c + 2 * i + 2, :]

    def land_rows(c, field, k):
        above1, below1 = rows_r[k, 0, c].astype(F32), rows_r[k, 1, c].astype(F32)
        above2, below2 = rows_r[k, 2, c].astype(F32), rows_r[k, 3, c].astype(F32)
        above = above1 * a1 + above2 * a2
        below = below1 * b1 + below2 * b2
        for i in range(2):
            cut = slice(i * BROAD, (i + 1) * BROAD)
            field[c, pl.ds(i * PITCH + 8, BROAD), :] = above[cut]
            field[c, pl.ds((10 + i) * PITCH + 8, BROAD), :] = below[cut]
            field[c, pl.ds(i * PITCH + 40, 2), :] = above1[i * BROAD:i * BROAD + 2] * (has_a * has_r)
            field[c, pl.ds((10 + i) * PITCH + 6, 2), :] = below1[i * BROAD + 30:i * BROAD + 32] * (has_b * has_l)

    def land_cols(c, field, k):
        left = cols_r[k, 0, c].astype(F32) * has_l
        right = cols_r[k, 1, c].astype(F32) * has_r
        for i in range(2):
            field[c, pl.ds(2 * PITCH + 6 + i, 8, stride=PITCH), :] = left[i * 8:(i + 1) * 8]
            field[c, pl.ds(2 * PITCH + 40 + i, 8, stride=PITCH), :] = right[i * 8:(i + 1) * 8]

    def convolve(c, field, flipped, put, starts):
        taps = [dwk[c, pl.ds(t, 1), :] for t in range(25)]
        for y in starts:
            acc = [None, None]
            for r in range(6):
                for b in range(5):
                    rows = field[c, pl.ds((y + r) * PITCH + 6 + b, BROAD), :]
                    for k in range(2):
                        a = r - k
                        if 0 <= a < 5:
                            t = 24 - (5 * a + b) if flipped else 5 * a + b
                            term = rows * taps[t]
                            acc[k] = term if acc[k] is None else acc[k] + term
            for k in range(2):
                put(c, y + k, acc[k])

    def post_state(e, j, state, key_sum):
        if STATE_DT == F32:
            tail = jnp.broadcast_to(key_sum, (8, LANES))
        else:
            row = lax.broadcasted_iota(jnp.int32, (8, LANES), 0)
            high = key_sum.astype(BF16).astype(F32)
            tail = jnp.where(row == 0, high, jnp.where(row == 1, key_sum - high, 0.0))
        for r in range(4):
            st_send[e, 4 * j + r] = jnp.concatenate([state[8 * r:8 * r + 8], tail], axis=0).astype(STATE_DT)

    def rs(e, d):
        p = peer(d)
        return push(st_send.at[e, p], st_recv.at[e, me], rs_s.at[e, d], rs_r.at[e, me], {"tile": p})

    def rs_from(e, d):
        p = peer(d)
        return push(st_send.at[e, p], st_recv.at[e, p], rs_s.at[e, d], rs_r.at[e, p], {"tile": p})

    def ag(e, d):
        p = peer(d)
        return push(st_tot.at[e, p], st_out.at[e, me], ag_s.at[e, d], ag_r.at[e, me], {"tile": p})

    def ag_from(e, d):
        p = peer(d)
        return push(st_tot.at[e, p], st_out.at[e, p], ag_s.at[e, d], ag_r.at[e, p], {"tile": p})

    def scatter(e):
        far_first(TILES, lambda d: rs(e, d).start())
        st_recv[e, me] = st_send[e, me]

    def total(e):
        loop(1, TILES, lambda d: rs_from(e, d).wait_recv())
        part = [st_recv[e, s].astype(F32) for s in range(TILES)]
        ahead, behind = [part[0]], [jnp.zeros_like(part[0])]
        for s in range(1, TILES):
            ahead.append(ahead[-1] * keep[s] + part[s])
            behind.append((behind[-1] + part[TILES - s]) * keep[TILES - s])
        for s in range(TILES):
            run = ahead[s] + behind[TILES - 1 - s]
            if STATE_DT == F32:
                st_tot[e, s] = run
            else:
                row = lax.broadcasted_iota(jnp.int32, (8, LANES), 0)
                key_sum = run[8:9] + run[9:10]
                high = key_sum.astype(BF16).astype(F32)
                tail = jnp.where(row == 0, high, jnp.where(row == 1, key_sum - high, 0.0))
                st_tot[e, s] = jnp.concatenate([run[0:8], tail], axis=0).astype(STATE_DT)
        far_first(TILES, lambda d: ag(e, d).start())
        st_out[e, me] = st_tot[e, me]

    def gather(e):
        loop(1, TILES, lambda d: ag_from(e, d).wait_recv())

    def get_state(e, j):
        parts = [st_out[e, 4 * j + r].astype(F32) for r in range(4)]
        state = expand(jnp.concatenate([part[0:8] for part in parts], axis=0))
        key_sum = parts[0][8:9]
        if STATE_DT != F32:
            key_sum = key_sum + parts[0][9:10]
        return (split(state) if STATE_DT == F32 else (state.astype(BF16),)), key_sum

    def terms(scale, j):
        if scale == 0:
            raw = x_raw[j]
            return raw.astype(F32), (raw,)
        raw = mrg[j]
        return raw, split(raw)

    def relu_terms(scale, j):
        raw, parts = terms(scale, j)
        rect = jnp.maximum(raw, 0.0)
        return raw, rect, ((rect.astype(BF16),) if scale == 0 else split(rect))

    def states(scale):
        def body(j):
            _, rect, keys = relu_terms(scale, 4 + j)
            _, values = terms(scale, 8 + j)
            post_state(scale, j, compact(mm(keys, values, TN)), jnp.sum(rect, axis=0, keepdims=True))
        loop(0, 4, body)

    def attend(scale, grads):
        def body(j):
            state, key_sum = get_state(scale, j)
            raw, rect, queries = relu_terms(scale, j)
            den = mm(split(rect * key_sum), same_bf, NN) + EPSILON
            inverse = 1.0 / den
            num = mm(queries, state, NN)
            grad = c_in[4 * scale + j].astype(F32)
            grad_num = grad * inverse
            grad_den = -mm(split(grad_num * num), same_bf, NN) * inverse
            grad_parts = split(grad_num)
            grad_query = mm(grad_parts, state, NT) + grad_den * key_sum
            grads[j] = jnp.where(raw > 0, grad_query, 0.0)
            post_state(2 + scale, j, compact(mm(queries, grad_parts, TN)),
                       jnp.sum(rect * grad_den, axis=0, keepdims=True))
        loop(0, 4, body)

    def attend_back(scale, grads):
        def body(j):
            state, key_sum = get_state(2 + scale, j)
            raw, _, keys = relu_terms(scale, 4 + j)
            _, values = terms(scale, 8 + j)
            grad_key = mm(values, state, NT) + key_sum
            grads[4 + j] = jnp.where(raw > 0, grad_key, 0.0)
            grads[8 + j] = mm(keys, state, NN)
        loop(0, 4, body)

    loop(0, NB, lambda c: stage(c, pad, 0))
    stage_corners(pad, 0, 0, NB)
    pl.semaphore_wait(barrier, (TILES - 1) + (nx - 1) + (ny - 1))
    halo_q, halo_k, halo_v = (halo(0, lo, lo + QB) for lo in (0, QB, 2 * QB))
    for copy in halo_k[:4] + halo_v[:4] + halo_k[4:] + halo_v[4:]:
        copy.start()
    states(0)
    scatter(0)
    for copy in halo_q:
        copy.start()

    for copy in meta:
        copy.wait()
    slots = im_h.shape[1]
    tall, wide, first, end = (jnp.int32(0) for _ in range(4))
    ends = []
    for m in range(slots):
        start = end
        end = end + im_h[0, m] * im_w[0, m]
        mine = (start <= me) & (me < end)
        tall = tall + jnp.where(mine, im_h[0, m], 0)
        wide = wide + jnp.where(mine, im_w[0, m], 0)
        first = first + jnp.where(mine, start, 0)
        ends.append(end)
    live = flag(me < end)
    within = me - first
    col = jnp.where(wide == 2, within % 2, 0)
    row = jnp.where(wide == 2, within // 2, within)
    has_l = live * flag(col > 0)
    has_r = live * flag(col < wide - 1)
    has_a = live * flag(row > 0)
    has_b = live * flag(row < tall - 1)
    thin = flag(wide == 1)
    a1, a2, b1, b2 = has_a * thin, has_a * (one - thin), has_b * thin, has_b * (one - thin)
    keep = [zero] * TILES
    for s in range(1, TILES):
        joined = one
        for m in range(slots):
            joined = joined * flag(ends[m] != s)
        keep[s] = joined

    for c in range(NB):
        lanes = pl.ds(c * LANES, LANES)
        pltpu.make_async_copy(dw.at[:, lanes], dwk.at[c], in_sem.at[NB + c]).wait()
        pltpu.make_async_copy(pw.at[:, lanes], pwk.at[c], in_sem.at[2 * NB + c]).wait()
    for c in range(8):
        pltpu.make_async_copy(cot.at[:, pl.ds(c * LANES, LANES)], c_in.at[c], in_sem.at[3 * NB + c]).wait()

    def put_mix(c, y, rows):
        mix[c, y * BROAD:(y + 1) * BROAD, :] = rows

    def inner(c):
        land_cols(c, pad, 0)
        convolve(c, pad, False, put_mix, (2, 4))

    def outer(c):
        land_rows(c, pad, 0)
        convolve(c, pad, False, put_mix, (0, 6))
        m_hi[c], m_lo[c] = split(mix[c])
        mrg[c] = mm((m_hi[c], m_lo[c]), (w_hi[c], w_lo[c]), NN)

    def weigh(c):
        w_hi[c], w_lo[c] = split(expand(pwk[c]))

    loop(0, NB, weigh)
    for copy in halo_k[:4] + halo_v[:4]:
        copy.wait_recv()
    land_corners(pad, 0, QB, NB)
    loop(QB, NB, inner)
    for copy in halo_k[4:]:
        copy.wait_recv()
    loop(QB, 2 * QB, outer)
    for copy in halo_v[4:]:
        copy.wait_recv()
    loop(2 * QB, NB, outer)
    states(1)
    scatter(1)
    total(0)
    for copy in halo_q:
        copy.wait_recv()
    land_corners(pad, 0, 0, QB)
    loop(0, QB, lambda c: (inner(c), outer(c)))
    total(1)
    gather(0)
    attend(0, gsrc)
    scatter(2)
    gather(1)
    attend(1, gmrg)
    scatter(3)
    total(2)

    dw_tmp[...] = jnp.zeros((32, LANES), F32)

    def backward(c):
        grads = split(gmrg[c] * live)
        grad_mix = mm(grads, (w_hi[c], w_lo[c]), NT)
        for y in range(TALL):
            pad2[c, pl.ds((2 + y) * PITCH + 8, BROAD), :] = grad_mix[y * BROAD:(y + 1) * BROAD]
        rows_s[0, c] = grad_mix[POS - 64:].astype(BF16)
        rows_s[1, c] = grad_mix[:64].astype(BF16)
        stage(c, pad2, 1)
        grad_pw = compact(mm((m_hi[c], m_lo[c]), grads, TN))
        for b in range(5):
            acc = [None] * 5
            for r in range(12):
                rows = pad[c, pl.ds(r * PITCH + 6 + b, BROAD), :]
                for a in range(5):
                    y = r - a
                    if 0 <= y < TALL:
                        term = rows * pad2[c, pl.ds((2 + y) * PITCH + 8, BROAD), :]
                        term = (term[0:8] + term[8:16]) + (term[16:24] + term[24:32])
                        acc[a] = term if acc[a] is None else acc[a] + term
            for a in range(5):
                t = 5 * a + b
                dw_tmp[t:t + 1, :] = jnp.sum(acc[a], axis=0, keepdims=True)
        for i in range(2):
            g_send[4 * c + i] = grad_pw[16 * i:16 * i + 16].astype(GRAD_DT)
            g_send[4 * c + 2 + i] = dw_tmp[16 * i:16 * i + 16, :].astype(GRAD_DT)

    def add_up(ref, count, lo, n):
        acc = ref[0, lo:lo + n].astype(F32)
        for s in range(1, count):
            acc = acc + ref[s, lo:lo + n].astype(F32)
        return acc

    class Part:
        def __init__(self, k, first, lo, n):
            self.k, self.first, self.lo, self.n = k, first, lo, n
            self.cut = pl.ds(lo, n)

        def piece(self, p):
            return pl.ds(self.first + self.n * p, self.n)

        def rs(self, d, slot_of):
            p = peer(d)
            return push(g_send.at[self.piece(p)], g_recv.at[slot_of, self.cut],
                        gr_s.at[self.k, d], gr_r.at[self.k, slot_of], {"tile": p})

        def x(self, d, slot_of):
            return push(g_x.at[mx, self.cut], g_x.at[slot_of, self.cut],
                        gx_s.at[self.k, d], gx_r.at[self.k, slot_of], {"img": x_peer(d)})

        def y(self, d, slot_of):
            return push(g_y.at[my, self.cut], g_y.at[slot_of, self.cut],
                        gy_s.at[self.k, d], gy_r.at[self.k, slot_of], {"img": y_peer(d)})

        def ag(self, d, slot_of):
            return push(g_tot.at[self.cut], g_all.at[self.piece(slot_of)],
                        ga_s.at[self.k, d], ga_r.at[self.k, slot_of], {"tile": peer(d)})

        def scatter(self):
            far_first(TILES, lambda d: self.rs(d, me).start())
            g_recv[me, self.lo:self.lo + self.n] = g_send[self.piece(me)]

        def send_x(self):
            loop(1, TILES, lambda d: self.rs(d, peer(d)).wait_recv())
            g_x[mx, self.lo:self.lo + self.n] = add_up(g_recv, TILES, self.lo, self.n)
            if nx > 1:
                far_first(nx, lambda d: self.x(d, mx).start())

        def send_y(self):
            if nx > 1:
                loop(1, nx, lambda d: self.x(d, lax.rem(mx + d, nx)).wait_recv())
            g_y[my, self.lo:self.lo + self.n] = add_up(g_x, nx, self.lo, self.n).astype(GRAD_DT)
            if ny > 1:
                far_first(ny, lambda d: self.y(d, my).start())

        def send_all(self):
            if ny > 1:
                loop(1, ny, lambda d: self.y(d, lax.rem(my + d, ny)).wait_recv())
            g_tot[self.lo:self.lo + self.n] = (add_up(g_y, ny, self.lo, self.n) * norm).astype(GRAD_DT)
            far_first(TILES, lambda d: self.ag(d, me).start())
            g_all[self.piece(me)] = g_tot[self.lo:self.lo + self.n]

        def finish(self):
            loop(1, TILES, lambda d: self.ag(d, peer(d)).wait_recv())

        def drain(self):
            def body(d):
                self.rs(d, me).wait_send()
                self.ag(d, me).wait_send()
            loop(1, TILES, body)
            if nx > 1:
                loop(1, nx, lambda d: self.x(d, mx).wait_send())
            if ny > 1:
                loop(1, ny, lambda d: self.y(d, my).wait_send())

    part_q, part_k, part_v = (Part(k, 16 * k, k, 1) for k in range(3))

    def put_out(c, y, rows):
        rows = (rows + gsrc[c, y * BROAD:(y + 1) * BROAD, :]) * live
        lanes = pl.ds(pl.multiple_of(c * LANES, LANES), LANES)
        out[y * BROAD:(y + 1) * BROAD, lanes] = rows.astype(BF16)

    def last(c):
        land_cols(c, pad2, 1)
        land_rows(c, pad2, 1)
        convolve(c, pad2, True, put_out, (0, 2, 4, 6))

    back_q, back_k, back_v = (halo(1, lo, lo + QB) for lo in (0, QB, 2 * QB))

    def send_back(copies, lo):
        stage_corners(pad2, 1, lo, lo + QB)
        for copy in copies:
            copy.start()

    def finish_back(copies, lo):
        for copy in copies:
            copy.wait_recv()
        land_corners(pad2, 1, lo, lo + QB)
        loop(lo, lo + QB, last)

    loop(0, QB, backward)
    part_q.scatter()
    total(3)
    send_back(back_q, 0)
    gather(2)
    attend_back(0, gsrc)
    part_q.send_x()
    gather(3)
    attend_back(1, gmrg)
    loop(QB, 2 * QB, backward)
    part_k.scatter()
    part_q.send_y()
    loop(2 * QB, NB, backward)
    part_v.scatter()
    send_back(back_k, QB)
    send_back(back_v, 2 * QB)
    part_k.send_x()
    part_q.send_all()
    part_v.send_x()
    part_k.send_y()
    finish_back(back_q, 0)
    part_v.send_y()
    finish_back(back_k, QB)
    part_k.send_all()
    finish_back(back_v, 2 * QB)
    part_v.send_all()

    for copy in halo_q + halo_k + halo_v + back_q + back_k + back_v:
        copy.wait_send()

    def drain(d):
        for e in range(4):
            rs(e, d).wait_send()
            ag(e, d).wait_send()

    loop(1, TILES, drain)
    for part in (part_q, part_k, part_v):
        part.finish()
    for part in (part_q, part_k, part_v):
        part.drain()
    g_fin[...] = g_all[...]


def write(grad, sums, out, gdw, gpw, out_sem):
    copy = pltpu.make_async_copy(grad, out, out_sem)
    copy.start()
    for c in range(NB):
        lanes = slice(c * LANES, (c + 1) * LANES)
        for i in range(2):
            gpw[16 * i:16 * i + 16, lanes] = sums[4 * c + i].astype(F32)
        gdw[0:16, lanes] = sums[4 * c + 2].astype(F32)
        gdw[16:25, lanes] = sums[4 * c + 3].astype(F32)[0:9]
    copy.wait()


def local(nx, ny, qkv, cotangent, dw_weight, pw_weight, tile_image, tile_row, tile_col, image_height, image_width):
    channels, inner = qkv.shape[4], cotangent.shape[4]
    norm = 1.0 / math.sqrt(POS * lax.axis_size("tile") * lax.axis_size("img"))
    dma = pltpu.SemaphoreType.DMA
    vm = pltpu.VMEM
    hbm_spec = pl.BlockSpec(memory_space=pltpu.HBM)
    vmem = pl.BlockSpec(memory_space=pltpu.VMEM)
    scratch = [
        vm((NB, POS, LANES), BF16), vm((8, POS, LANES), BF16),
        vm((NB, POS, LANES), BF16), vm((NB, POS, LANES), BF16), vm((NB, LANES, LANES), BF16), vm((NB, LANES, LANES), BF16),
        vm((NB, 25, LANES), F32), vm((NB, HD, LANES), F32),
        vm((NB, 12 * PITCH, LANES), F32), vm((NB, 12 * PITCH, LANES), F32),
        vm((NB, POS, LANES), F32), vm((NB, POS, LANES), F32), vm((NB, POS, LANES), F32), vm((NB, POS, LANES), F32),
        pltpu.SMEM(image_height.shape, jnp.int32), pltpu.SMEM(image_width.shape, jnp.int32),
        vm((4, TILES, 16, LANES), STATE_DT), vm((4, TILES, 16, LANES), STATE_DT),
        vm((4, TILES, 16, LANES), STATE_DT), vm((4, TILES, 16, LANES), STATE_DT),
        vm((16, LANES), F32), vm((48, LANES), F32),
        vm((2, 2, NB, 16, LANES), BF16), vm((2, 2, 48, LANES), BF16), vm((2, NB, 64, LANES), BF16),
        vm((2, 4, NB, 64, LANES), BF16), vm((2, 2, NB, 16, LANES), BF16), vm((2, 2, 48, LANES), BF16),
        vm((32, LANES), F32),
        vm((48, 16, LANES), GRAD_DT), vm((TILES, 3, 16, LANES), GRAD_DT),
        vm((nx, 3, 16, LANES), F32), vm((ny, 3, 16, LANES), GRAD_DT),
        vm((3, 16, LANES), GRAD_DT), vm((48, 16, LANES), GRAD_DT),
        dma((3 * NB + 8,)), dma((2,)),
        dma((4, TILES)), dma((4, TILES)), dma((4, TILES)), dma((4, TILES)),
        dma((2, 3, 8)), dma((2, 3, 8)),
        dma((3, TILES)), dma((3, TILES)), dma((3, nx)), dma((3, nx)), dma((3, ny)), dma((3, ny)),
        dma((3, TILES)), dma((3, TILES)),
    ]
    grad, sums = pl.pallas_call(
        functools.partial(kernel, nx, ny, norm),
        out_shape=(jax.ShapeDtypeStruct((POS, channels), BF16), jax.ShapeDtypeStruct((4 * NB, 16, LANES), GRAD_DT)),
        in_specs=[hbm_spec] * 6,
        out_specs=(vmem, vmem),
        scratch_shapes=scratch,
        compiler_params=pltpu.CompilerParams(
            collective_id=0, has_side_effects=True, vmem_limit_bytes=40 * 1024 * 1024
        ),
        name="linear_attention",
    )(
        *[pltpu.with_memory_space_constraint(x, pltpu.HBM) for x in (
            qkv.reshape(POS, channels), cotangent.reshape(POS, inner), dw_weight, pw_weight,
            image_height, image_width)]
    )
    grad, grad_dw, grad_pw = pl.pallas_call(
        write,
        out_shape=(
            jax.ShapeDtypeStruct((POS, channels), BF16),
            jax.ShapeDtypeStruct((25, channels), F32),
            jax.ShapeDtypeStruct((HD, channels), F32),
        ),
        in_specs=[vmem, vmem],
        out_specs=(hbm_spec, vmem, vmem),
        scratch_shapes=[dma(())],
        compiler_params=pltpu.CompilerParams(vmem_limit_bytes=8 * 1024 * 1024),
        name="write_outputs",
    )(grad, sums)
    return grad.reshape(qkv.shape), grad_dw, grad_pw


def solution(mesh):
    placed = (
        P("img", "tile", None, None, None),
        P("img", "tile", None, None, None),
        P(),
        P(),
        P("img", "tile"),
        P("img", "tile"),
        P("img", "tile"),
        P("img", None),
        P("img", None),
    )
    count = mesh.shape["img"]
    nx = {32: 4, 4: 2}.get(count, 1)
    return jax.shard_map(
        functools.partial(local, nx, count // nx),
        mesh=mesh,
        in_specs=placed,
        out_specs=(P("img", "tile", None, None, None), P(), P()),
        check_vma=False,
    )
```

```python
import functools
import math

import jax
import jax.numpy as jnp
from jax import lax
from jax.experimental import pallas as pl
from jax.experimental.pallas import tpu as pltpu
from jax.sharding import PartitionSpec as P

MESH = pl.DeviceIdType.MESH
F32, BF16 = jnp.float32, jnp.bfloat16
EPSILON = 1e-06
TALL, BROAD, LANES, HD = 8, 32, 128, 32
POS = TALL * BROAD
PITCH = 48
NB = 12
TILES = 16
STATE_DT = BF16
GRAD_DT = BF16
QB = 4


def split(x):
    hi = x.astype(BF16)
    return hi, (x - hi.astype(F32)).astype(BF16)


def dot(a, b, dims):
    return lax.dot_general(a, b, (dims, ((), ())), preferred_element_type=F32)


NN, NT, TN = ((1,), (0,)), ((1,), (1,)), ((0,), (0,))


def mm(a, b, dims):
    out = dot(a[0], b[0], dims)
    if len(b) > 1:
        out = out + dot(a[0], b[1], dims)
    if len(a) > 1:
        out = out + dot(a[1], b[0], dims)
    return out


def kernel(nx, ny, norm, qkv, cot, dw, pw, im_h_in, im_w_in, out, g_fin, *scratch):
    (x_raw, c_in, m_hi, m_lo, w_hi, w_lo, dwk, pwk, pad, pad2, mix, mrg, gsrc, gmrg, im_h, im_w,
     st_send, st_recv, st_tot, st_out,
     cols_f, corner_f, cols_s, corner_s, rows_s, rows_r, cols_r, corner_r,
     dw_tmp, g_send, g_recv, g_x, g_y, g_tot, g_all,
     in_sem, meta_sem, rs_s, rs_r, ag_s, ag_r, h_s, h_r, gr_s, gr_r, gx_s, gx_r, gy_s, gy_r, ga_s, ga_r) = scratch
    me = lax.axis_index("tile")
    im = lax.axis_index("img")
    mx, my = lax.div(im, ny), lax.rem(im, ny)

    def peer(d):
        return lax.rem(me + (d + TILES), TILES)

    def x_peer(d):
        return lax.rem(mx + d, nx) * ny + my

    def y_peer(d):
        return mx * ny + lax.rem(my + d, ny)

    def push(src, dst, ssem, rsem, where):
        return pltpu.make_async_remote_copy(
            src_ref=src, dst_ref=dst, send_sem=ssem, recv_sem=rsem, device_id=where, device_id_type=MESH
        )

    def loop(lo, hi, body):
        lax.fori_loop(lo, hi, lambda i, carry: (body(i), carry)[1], 0)

    def far_first(count, body):
        half = count // 2
        body(half)
        loop(1, half, lambda h: (body(half - h), body(half + h)))

    def in_copies():
        copies = []
        for c in range(NB):
            lanes = pl.ds(c * LANES, LANES)
            copies.append(pltpu.make_async_copy(qkv.at[:, lanes], x_raw.at[c], in_sem.at[c]))
        for c in range(NB):
            lanes = pl.ds(c * LANES, LANES)
            copies.append(pltpu.make_async_copy(pw.at[:, lanes], pwk.at[c], in_sem.at[2 * NB + c]))
            copies.append(pltpu.make_async_copy(dw.at[:, lanes], dwk.at[c], in_sem.at[NB + c]))
        for c in range(8):
            lanes = pl.ds(c * LANES, LANES)
            copies.append(pltpu.make_async_copy(cot.at[:, lanes], c_in.at[c], in_sem.at[3 * NB + c]))
        return copies

    meta = [
        pltpu.make_async_copy(src, dst, meta_sem.at[i])
        for i, (src, dst) in enumerate(
            ((im_h_in, im_h), (im_w_in, im_w)))
    ]
    for copy in meta + in_copies():
        copy.start()

    barrier = pltpu.get_barrier_semaphore()
    far_first(TILES, lambda d: pl.semaphore_signal(
        barrier, inc=1, device_id={"tile": peer(d)}, device_id_type=MESH))
    if nx > 1:
        far_first(nx, lambda d: pl.semaphore_signal(
            barrier, inc=1, device_id={"img": x_peer(d)}, device_id_type=MESH))
    if ny > 1:
        far_first(ny, lambda d: pl.semaphore_signal(
            barrier, inc=1, device_id={"img": y_peer(d)}, device_id_type=MESH))

    one, zero = jnp.float32(1), jnp.float32(0)

    def flag(cond):
        return jnp.where(cond, one, zero)

    lane_head = lax.broadcasted_iota(jnp.int32, (LANES, LANES), 1) // HD
    row_head = lax.broadcasted_iota(jnp.int32, (LANES, LANES), 0) // HD
    same_head = flag(lane_head == row_head)
    same_bf = (same_head.astype(BF16),)

    def expand(compact):
        return jnp.concatenate([compact] * 4, axis=0) * same_head

    def compact(full):
        masked = full * same_head
        return masked[0:32] + masked[32:64] + masked[64:96] + masked[96:128]

    def place(c):
        pltpu.make_async_copy(qkv.at[:, pl.ds(0, LANES)], x_raw.at[c], in_sem.at[c]).wait()
        for y in range(TALL):
            rows = x_raw[c, y * BROAD:(y + 1) * BROAD, :].astype(F32)
            pad[c, pl.ds((2 + y) * PITCH + 8, BROAD), :] = rows

    loop(0, NB, place)

    def stage(c, field, k):
        for side, first in ((0, 38), (1, 8)):
            for i in range(2):
                cols_f[i * 8:(i + 1) * 8, :] = field[c, pl.ds(2 * PITCH + first + i, 8, stride=PITCH), :]
            cols_s[k, side, c] = cols_f[...].astype(BF16)

    def stage_corners(field, k, lo, hi):
        for side, row, first in ((0, 8, 38), (1, 2, 8)):
            for c in range(lo, hi):
                for i in range(2):
                    corner_f[4 * c + 2 * i:4 * c + 2 * i + 2, :] = field[c, pl.ds((row + i) * PITCH + first, 2), :]
            corner_s[k, side, 4 * lo:4 * hi] = corner_f[4 * lo:4 * hi, :].astype(BF16)

    def halo(k, lo, hi):
        blocks, group = pl.ds(lo, hi - lo), lo // QB
        corner = pl.ds(4 * lo, 4 * (hi - lo))
        if k == 0:
            bottom, top = x_raw.at[blocks, pl.ds(POS - 64, 64)], x_raw.at[blocks, pl.ds(0, 64)]
        else:
            bottom, top = rows_s.at[0, blocks], rows_s.at[1, blocks]
        plan = [
            (cols_s.at[k, 0, blocks], cols_r.at[k, 0, blocks], 1), (cols_s.at[k, 1, blocks], cols_r.at[k, 1, blocks], -1),
            (corner_s.at[k, 0, corner], corner_r.at[k, 0, corner], 3),
            (corner_s.at[k, 1, corner], corner_r.at[k, 1, corner], -3),
            (bottom, rows_r.at[k, 2, blocks], 2), (top, rows_r.at[k, 3, blocks], -2),
            (bottom, rows_r.at[k, 0, blocks], 1), (top, rows_r.at[k, 1, blocks], -1),
        ]
        return [
            push(src, dst, h_s.at[k, group, i], h_r.at[k, group, i], {"tile": peer(step)})
            for i, (src, dst, step) in enumerate(plan)
        ]

    def land_corners(field, k, lo, hi):
        for side, row, first, has in ((0, 0, 6, has_a * has_l), (1, 10, 40, has_b * has_r)):
            corner_f[4 * lo:4 * hi, :] = corner_r[k, side, 4 * lo:4 * hi].astype(F32) * has
            for c in range(lo, hi):
                for i in range(2):
                    field[c, pl.ds((row + i) * PITCH + first, 2), :] = corner_f[4 * c + 2 * i:4 * c + 2 * i + 2, :]

    def land_rows(c, field, k):
        above1, below1 = rows_r[k, 0, c].astype(F32), rows_r[k, 1, c].astype(F32)
        above2, below2 = rows_r[k, 2, c].astype(F32), rows_r[k, 3, c].astype(F32)
        above = above1 * a1 + above2 * a2
        below = below1 * b1 + below2 * b2
        for i in range(2):
            cut = slice(i * BROAD, (i + 1) * BROAD)
            field[c, pl.ds(i * PITCH + 8, BROAD), :] = above[cut]
            field[c, pl.ds((10 + i) * PITCH + 8, BROAD), :] = below[cut]
            field[c, pl.ds(i * PITCH + 40, 2), :] = above1[i * BROAD:i * BROAD + 2] * (has_a * has_r)
            field[c, pl.ds((10 + i) * PITCH + 6, 2), :] = below1[i * BROAD + 30:i * BROAD + 32] * (has_b * has_l)

    def land_cols(c, field, k):
        left = cols_r[k, 0, c].astype(F32) * has_l
        right = cols_r[k, 1, c].astype(F32) * has_r
        for i in range(2):
            field[c, pl.ds(2 * PITCH + 6 + i, 8, stride=PITCH), :] = left[i * 8:(i + 1) * 8]
            field[c, pl.ds(2 * PITCH + 40 + i, 8, stride=PITCH), :] = right[i * 8:(i + 1) * 8]

    def convolve(c, field, flipped, put, starts):
        taps = [dwk[c, pl.ds(t, 1), :] for t in range(25)]
        for y in starts:
            acc = [None, None]
            for r in range(6):
                for b in range(5):
                    rows = field[c, pl.ds((y + r) * PITCH + 6 + b, BROAD), :]
                    for k in range(2):
                        a = r - k
                        if 0 <= a < 5:
                            t = 24 - (5 * a + b) if flipped else 5 * a + b
                            term = rows * taps[t]
                            acc[k] = term if acc[k] is None else acc[k] + term
            for k in range(2):
                put(c, y + k, acc[k])

    def post_state(e, j, state, key_sum):
        if STATE_DT == F32:
            tail = jnp.broadcast_to(key_sum, (8, LANES))
        else:
            row = lax.broadcasted_iota(jnp.int32, (8, LANES), 0)
            high = key_sum.astype(BF16).astype(F32)
            tail = jnp.where(row == 0, high, jnp.where(row == 1, key_sum - high, 0.0))
        for r in range(4):
            st_send[e, 4 * j + r] = jnp.concatenate([state[8 * r:8 * r + 8], tail], axis=0).astype(STATE_DT)

    def rs(e, d):
        p = peer(d)
        return push(st_send.at[e, p], st_recv.at[e, me], rs_s.at[e, d], rs_r.at[e, me], {"tile": p})

    def rs_from(e, d):
        p = peer(d)
        return push(st_send.at[e, p], st_recv.at[e, p], rs_s.at[e, d], rs_r.at[e, p], {"tile": p})

    def ag(e, d):
        p = peer(d)
        return push(st_tot.at[e, p], st_out.at[e, me], ag_s.at[e, d], ag_r.at[e, me], {"tile": p})

    def ag_from(e, d):
        p = peer(d)
        return push(st_tot.at[e, p], st_out.at[e, p], ag_s.at[e, d], ag_r.at[e, p], {"tile": p})

    def scatter(e):
        far_first(TILES, lambda d: rs(e, d).start())
        st_recv[e, me] = st_send[e, me]

    def total(e):
        loop(1, TILES, lambda d: rs_from(e, d).wait_recv())
        part = [st_recv[e, s].astype(F32) for s in range(TILES)]
        ahead, behind = [part[0]], [jnp.zeros_like(part[0])]
        for s in range(1, TILES):
            ahead.append(ahead[-1] * keep[s] + part[s])
            behind.append((behind[-1] + part[TILES - s]) * keep[TILES - s])
        for s in range(TILES):
            run = ahead[s] + behind[TILES - 1 - s]
            if STATE_DT == F32:
                st_tot[e, s] = run
            else:
                row = lax.broadcasted_iota(jnp.int32, (8, LANES), 0)
                key_sum = run[8:9] + run[9:10]
                high = key_sum.astype(BF16).astype(F32)
                tail = jnp.where(row == 0, high, jnp.where(row == 1, key_sum - high, 0.0))
                st_tot[e, s] = jnp.concatenate([run[0:8], tail], axis=0).astype(STATE_DT)
        far_first(TILES, lambda d: ag(e, d).start())
        st_out[e, me] = st_tot[e, me]

    def gather(e):
        loop(1, TILES, lambda d: ag_from(e, d).wait_recv())

    def get_state(e, j):
        parts = [st_out[e, 4 * j + r].astype(F32) for r in range(4)]
        state = expand(jnp.concatenate([part[0:8] for part in parts], axis=0))
        key_sum = parts[0][8:9]
        if STATE_DT != F32:
            key_sum = key_sum + parts[0][9:10]
        return (split(state) if STATE_DT == F32 else (state.astype(BF16),)), key_sum

    def terms(scale, j):
        if scale == 0:
            raw = x_raw[j]
            return raw.astype(F32), (raw,)
        raw = mrg[j]
        return raw, split(raw)

    def relu_terms(scale, j):
        raw, parts = terms(scale, j)
        rect = jnp.maximum(raw, 0.0)
        return raw, rect, ((rect.astype(BF16),) if scale == 0 else split(rect))

    def states(scale):
        def body(j):
            _, rect, keys = relu_terms(scale, 4 + j)
            _, values = terms(scale, 8 + j)
            post_state(scale, j, compact(mm(keys, values, TN)), jnp.sum(rect, axis=0, keepdims=True))
        for j in range(4):
            body(j)

    def attend(scale, grads):
        def body(j):
            state, key_sum = get_state(scale, j)
            raw, rect, queries = relu_terms(scale, j)
            den = mm(split(rect * key_sum), same_bf, NN) + EPSILON
            inverse = 1.0 / den
            num = mm(queries, state, NN)
            grad = c_in[4 * scale + j].astype(F32)
            grad_num = grad * inverse
            grad_den = -mm(split(grad_num * num), same_bf, NN) * inverse
            grad_parts = split(grad_num)
            grad_query = mm(grad_parts, state, NT) + grad_den * key_sum
            grads[j] = jnp.where(raw > 0, grad_query, 0.0)
            post_state(2 + scale, j, compact(mm(queries, grad_parts, TN)),
                       jnp.sum(rect * grad_den, axis=0, keepdims=True))
        for j in range(4):
            body(j)

    def attend_back(scale, grads):
        def body(j):
            state, key_sum = get_state(2 + scale, j)
            raw, _, keys = relu_terms(scale, 4 + j)
            _, values = terms(scale, 8 + j)
            grad_key = mm(values, state, NT) + key_sum
            grads[4 + j] = jnp.where(raw > 0, grad_key, 0.0)
            grads[8 + j] = mm(keys, state, NN)
        for j in range(4):
            body(j)

    loop(0, NB, lambda c: stage(c, pad, 0))
    stage_corners(pad, 0, 0, NB)
    pl.semaphore_wait(barrier, (TILES - 1) + (nx - 1) + (ny - 1))
    halo_q, halo_k, halo_v = (halo(0, lo, lo + QB) for lo in (0, QB, 2 * QB))
    for copy in halo_k[:4] + halo_v[:4] + halo_k[4:] + halo_v[4:]:
        copy.start()
    states(0)
    scatter(0)
    for copy in halo_q:
        copy.start()

    for copy in meta:
        copy.wait()
    slots = im_h.shape[1]
    tall, wide, first, end = (jnp.int32(0) for _ in range(4))
    ends = []
    for m in range(slots):
        start = end
        end = end + im_h[0, m] * im_w[0, m]
        mine = (start <= me) & (me < end)
        tall = tall + jnp.where(mine, im_h[0, m], 0)
        wide = wide + jnp.where(mine, im_w[0, m], 0)
        first = first + jnp.where(mine, start, 0)
        ends.append(end)
    live = flag(me < end)
    within = me - first
    col = jnp.where(wide == 2, within % 2, 0)
    row = jnp.where(wide == 2, within // 2, within)
    has_l = live * flag(col > 0)
    has_r = live * flag(col < wide - 1)
    has_a = live * flag(row > 0)
    has_b = live * flag(row < tall - 1)
    thin = flag(wide == 1)
    a1, a2, b1, b2 = has_a * thin, has_a * (one - thin), has_b * thin, has_b * (one - thin)
    keep = [zero] * TILES
    for s in range(1, TILES):
        joined = one
        for m in range(slots):
            joined = joined * flag(ends[m] != s)
        keep[s] = joined

    for c in range(NB):
        lanes = pl.ds(c * LANES, LANES)
        pltpu.make_async_copy(dw.at[:, lanes], dwk.at[c], in_sem.at[NB + c]).wait()
        pltpu.make_async_copy(pw.at[:, lanes], pwk.at[c], in_sem.at[2 * NB + c]).wait()
    for c in range(8):
        pltpu.make_async_copy(cot.at[:, pl.ds(c * LANES, LANES)], c_in.at[c], in_sem.at[3 * NB + c]).wait()

    def put_mix(c, y, rows):
        mix[c, y * BROAD:(y + 1) * BROAD, :] = rows

    def inner(c):
        land_cols(c, pad, 0)
        convolve(c, pad, False, put_mix, (2, 4))

    def outer(c):
        land_rows(c, pad, 0)
        convolve(c, pad, False, put_mix, (0, 6))
        m_hi[c], m_lo[c] = split(mix[c])
        mrg[c] = mm((m_hi[c], m_lo[c]), (w_hi[c], w_lo[c]), NN)

    def weigh(c):
        w_hi[c], w_lo[c] = split(expand(pwk[c]))

    loop(0, NB, weigh)
    for copy in halo_k[:4] + halo_v[:4]:
        copy.wait_recv()
    land_corners(pad, 0, QB, NB)
    loop(QB, NB, inner)
    for copy in halo_k[4:]:
        copy.wait_recv()
    loop(QB, 2 * QB, outer)
    for copy in halo_v[4:]:
        copy.wait_recv()
    loop(2 * QB, NB, outer)
    states(1)
    scatter(1)
    total(0)
    for copy in halo_q:
        copy.wait_recv()
    land_corners(pad, 0, 0, QB)
    loop(0, QB, lambda c: (inner(c), outer(c)))
    total(1)
    gather(0)
    attend(0, gsrc)
    scatter(2)
    gather(1)
    attend(1, gmrg)
    scatter(3)
    total(2)

    dw_tmp[...] = jnp.zeros((32, LANES), F32)

    def backward(c):
        grads = split(gmrg[c] * live)
        grad_mix = mm(grads, (w_hi[c], w_lo[c]), NT)
        for y in range(TALL):
            pad2[c, pl.ds((2 + y) * PITCH + 8, BROAD), :] = grad_mix[y * BROAD:(y + 1) * BROAD]
        rows_s[0, c] = grad_mix[POS - 64:].astype(BF16)
        rows_s[1, c] = grad_mix[:64].astype(BF16)
        stage(c, pad2, 1)
        grad_pw = compact(mm((m_hi[c], m_lo[c]), grads, TN))
        for b in range(5):
            acc = [None] * 5
            for r in range(12):
                rows = pad[c, pl.ds(r * PITCH + 6 + b, BROAD), :]
                for a in range(5):
                    y = r - a
                    if 0 <= y < TALL:
                        term = rows * pad2[c, pl.ds((2 + y) * PITCH + 8, BROAD), :]
                        term = (term[0:8] + term[8:16]) + (term[16:24] + term[24:32])
                        acc[a] = term if acc[a] is None else acc[a] + term
            for a in range(5):
                t = 5 * a + b
                dw_tmp[t:t + 1, :] = jnp.sum(acc[a], axis=0, keepdims=True)
        for i in range(2):
            g_send[4 * c + i] = grad_pw[16 * i:16 * i + 16].astype(GRAD_DT)
            g_send[4 * c + 2 + i] = dw_tmp[16 * i:16 * i + 16, :].astype(GRAD_DT)

    def add_up(ref, count, lo, n):
        acc = ref[0, lo:lo + n].astype(F32)
        for s in range(1, count):
            acc = acc + ref[s, lo:lo + n].astype(F32)
        return acc

    class Part:
        def __init__(self, k, first, lo, n):
            self.k, self.first, self.lo, self.n = k, first, lo, n
            self.cut = pl.ds(lo, n)

        def piece(self, p):
            return pl.ds(self.first + self.n * p, self.n)

        def rs(self, d, slot_of):
            p = peer(d)
            return push(g_send.at[self.piece(p)], g_recv.at[slot_of, self.cut],
                        gr_s.at[self.k, d], gr_r.at[self.k, slot_of], {"tile": p})

        def x(self, d, slot_of):
            return push(g_x.at[mx, self.cut], g_x.at[slot_of, self.cut],
                        gx_s.at[self.k, d], gx_r.at[self.k, slot_of], {"img": x_peer(d)})

        def y(self, d, slot_of):
            return push(g_y.at[my, self.cut], g_y.at[slot_of, self.cut],
                        gy_s.at[self.k, d], gy_r.at[self.k, slot_of], {"img": y_peer(d)})

        def ag(self, d, slot_of):
            return push(g_tot.at[self.cut], g_all.at[self.piece(slot_of)],
                        ga_s.at[self.k, d], ga_r.at[self.k, slot_of], {"tile": peer(d)})

        def scatter(self):
            far_first(TILES, lambda d: self.rs(d, me).start())
            g_recv[me, self.lo:self.lo + self.n] = g_send[self.piece(me)]

        def send_x(self):
            loop(1, TILES, lambda d: self.rs(d, peer(d)).wait_recv())
            g_x[mx, self.lo:self.lo + self.n] = add_up(g_recv, TILES, self.lo, self.n)
            if nx > 1:
                far_first(nx, lambda d: self.x(d, mx).start())

        def send_y(self):
            if nx > 1:
                loop(1, nx, lambda d: self.x(d, lax.rem(mx + d, nx)).wait_recv())
            g_y[my, self.lo:self.lo + self.n] = add_up(g_x, nx, self.lo, self.n).astype(GRAD_DT)
            if ny > 1:
                far_first(ny, lambda d: self.y(d, my).start())

        def send_all(self):
            if ny > 1:
                loop(1, ny, lambda d: self.y(d, lax.rem(my + d, ny)).wait_recv())
            g_tot[self.lo:self.lo + self.n] = (add_up(g_y, ny, self.lo, self.n) * norm).astype(GRAD_DT)
            far_first(TILES, lambda d: self.ag(d, me).start())
            g_all[self.piece(me)] = g_tot[self.lo:self.lo + self.n]

        def finish(self):
            loop(1, TILES, lambda d: self.ag(d, peer(d)).wait_recv())

        def drain(self):
            def body(d):
                self.rs(d, me).wait_send()
                self.ag(d, me).wait_send()
            loop(1, TILES, body)
            if nx > 1:
                loop(1, nx, lambda d: self.x(d, mx).wait_send())
            if ny > 1:
                loop(1, ny, lambda d: self.y(d, my).wait_send())

    part_q, part_k, part_v = (Part(k, 16 * k, k, 1) for k in range(3))

    def put_out(c, y, rows):
        rows = (rows + gsrc[c, y * BROAD:(y + 1) * BROAD, :]) * live
        lanes = pl.ds(pl.multiple_of(c * LANES, LANES), LANES)
        out[y * BROAD:(y + 1) * BROAD, lanes] = rows.astype(BF16)

    def last(c):
        land_cols(c, pad2, 1)
        land_rows(c, pad2, 1)
        convolve(c, pad2, True, put_out, (0, 2, 4, 6))

    back_q, back_k, back_v = (halo(1, lo, lo + QB) for lo in (0, QB, 2 * QB))

    def send_back(copies, lo):
        stage_corners(pad2, 1, lo, lo + QB)
        for copy in copies:
            copy.start()

    def finish_back(copies, lo):
        for copy in copies:
            copy.wait_recv()
        land_corners(pad2, 1, lo, lo + QB)
        loop(lo, lo + QB, last)

    loop(0, QB, backward)
    part_q.scatter()
    total(3)
    send_back(back_q, 0)
    gather(2)
    attend_back(0, gsrc)
    part_q.send_x()
    gather(3)
    attend_back(1, gmrg)
    loop(QB, 2 * QB, backward)
    part_k.scatter()
    part_q.send_y()
    loop(2 * QB, NB, backward)
    part_v.scatter()
    finish_back(back_q, 0)
    send_back(back_k, QB)
    send_back(back_v, 2 * QB)
    part_k.send_x()
    part_v.send_x()
    part_k.send_y()
    part_v.send_y()
    part_q.send_all()
    finish_back(back_k, QB)
    part_k.send_all()
    finish_back(back_v, 2 * QB)
    part_v.send_all()

    for copy in halo_q + halo_k + halo_v + back_q + back_k + back_v:
        copy.wait_send()

    def drain(d):
        for e in range(4):
            rs(e, d).wait_send()
            ag(e, d).wait_send()

    loop(1, TILES, drain)
    for part in (part_q, part_k, part_v):
        part.finish()
    for part in (part_q, part_k, part_v):
        part.drain()
    g_fin[...] = g_all[...]


def write(grad, sums, out, gdw, gpw, out_sem):
    copy = pltpu.make_async_copy(grad, out, out_sem)
    copy.start()
    for c in range(NB):
        lanes = slice(c * LANES, (c + 1) * LANES)
        for i in range(2):
            gpw[16 * i:16 * i + 16, lanes] = sums[4 * c + i].astype(F32)
        gdw[0:16, lanes] = sums[4 * c + 2].astype(F32)
        gdw[16:25, lanes] = sums[4 * c + 3].astype(F32)[0:9]
    copy.wait()


def local(nx, ny, qkv, cotangent, dw_weight, pw_weight, tile_image, tile_row, tile_col, image_height, image_width):
    channels, inner = qkv.shape[4], cotangent.shape[4]
    norm = 1.0 / math.sqrt(POS * lax.axis_size("tile") * lax.axis_size("img"))
    dma = pltpu.SemaphoreType.DMA
    vm = pltpu.VMEM
    hbm_spec = pl.BlockSpec(memory_space=pltpu.HBM)
    vmem = pl.BlockSpec(memory_space=pltpu.VMEM)
    scratch = [
        vm((NB, POS, LANES), BF16), vm((8, POS, LANES), BF16),
        vm((NB, POS, LANES), BF16), vm((NB, POS, LANES), BF16), vm((NB, LANES, LANES), BF16), vm((NB, LANES, LANES), BF16),
        vm((NB, 25, LANES), F32), vm((NB, HD, LANES), F32),
        vm((NB, 12 * PITCH, LANES), F32), vm((NB, 12 * PITCH, LANES), F32),
        vm((NB, POS, LANES), F32), vm((NB, POS, LANES), F32), vm((NB, POS, LANES), F32), vm((NB, POS, LANES), F32),
        pltpu.SMEM(image_height.shape, jnp.int32), pltpu.SMEM(image_width.shape, jnp.int32),
        vm((4, TILES, 16, LANES), STATE_DT), vm((4, TILES, 16, LANES), STATE_DT),
        vm((4, TILES, 16, LANES), STATE_DT), vm((4, TILES, 16, LANES), STATE_DT),
        vm((16, LANES), F32), vm((48, LANES), F32),
        vm((2, 2, NB, 16, LANES), BF16), vm((2, 2, 48, LANES), BF16), vm((2, NB, 64, LANES), BF16),
        vm((2, 4, NB, 64, LANES), BF16), vm((2, 2, NB, 16, LANES), BF16), vm((2, 2, 48, LANES), BF16),
        vm((32, LANES), F32),
        vm((48, 16, LANES), GRAD_DT), vm((TILES, 3, 16, LANES), GRAD_DT),
        vm((nx, 3, 16, LANES), F32), vm((ny, 3, 16, LANES), GRAD_DT),
        vm((3, 16, LANES), GRAD_DT), vm((48, 16, LANES), GRAD_DT),
        dma((3 * NB + 8,)), dma((2,)),
        dma((4, TILES)), dma((4, TILES)), dma((4, TILES)), dma((4, TILES)),
        dma((2, 3, 8)), dma((2, 3, 8)),
        dma((3, TILES)), dma((3, TILES)), dma((3, nx)), dma((3, nx)), dma((3, ny)), dma((3, ny)),
        dma((3, TILES)), dma((3, TILES)),
    ]
    grad, sums = pl.pallas_call(
        functools.partial(kernel, nx, ny, norm),
        out_shape=(jax.ShapeDtypeStruct((POS, channels), BF16), jax.ShapeDtypeStruct((4 * NB, 16, LANES), GRAD_DT)),
        in_specs=[hbm_spec] * 6,
        out_specs=(vmem, vmem),
        scratch_shapes=scratch,
        compiler_params=pltpu.CompilerParams(
            collective_id=0, has_side_effects=True, vmem_limit_bytes=40 * 1024 * 1024
        ),
        name="linear_attention",
    )(
        *[pltpu.with_memory_space_constraint(x, pltpu.HBM) for x in (
            qkv.reshape(POS, channels), cotangent.reshape(POS, inner), dw_weight, pw_weight,
            image_height, image_width)]
    )
    grad, grad_dw, grad_pw = pl.pallas_call(
        write,
        out_shape=(
            jax.ShapeDtypeStruct((POS, channels), BF16),
            jax.ShapeDtypeStruct((25, channels), F32),
            jax.ShapeDtypeStruct((HD, channels), F32),
        ),
        in_specs=[vmem, vmem],
        out_specs=(hbm_spec, vmem, vmem),
        scratch_shapes=[dma(())],
        compiler_params=pltpu.CompilerParams(vmem_limit_bytes=8 * 1024 * 1024),
        name="write_outputs",
    )(grad, sums)
    return grad.reshape(qkv.shape), grad_dw, grad_pw


def solution(mesh):
    placed = (
        P("img", "tile", None, None, None),
        P("img", "tile", None, None, None),
        P(),
        P(),
        P("img", "tile"),
        P("img", "tile"),
        P("img", "tile"),
        P("img", None),
        P("img", None),
    )
    count = mesh.shape["img"]
    nx = {32: 4, 4: 2}.get(count, 1)
    return jax.shard_map(
        functools.partial(local, nx, count // nx),
        mesh=mesh,
        in_specs=placed,
        out_specs=(P("img", "tile", None, None, None), P(), P()),
        check_vma=False,
    )
```
